32 devices in a mesh: dp: 2 (over x), expert: 16 (over z, y, core).
Axes of the slice: x: 2, y: 2, z: 4, core: 2. Of those that a mesh axis runs over, the one named last changes fastest.
Arguments:
- tokens: bfloat16 [512, 2048], P('expert', 'dp'), may hold values from -6 to 6
- cotangent: bfloat16 [512, 2048], P('expert', 'dp'), may hold values from -6 to 6
- routes: int32 [512, 8], P('expert'), may hold values from 0 to 15, all different within a row; in each aligned block of 32 rows (0 to 31, 32 to 63, ...) at most 20 rows name the same one
- probs: float32 [512, 8], P('expert'), may hold values from 0.03 to 0.6
- matching: int32 [16], replicated, may hold values from 0 to 15, as said below
- gate_weight: bfloat16 [16, 2048, 1024], P('expert', None, 'dp'), may hold values from -0.125 to 0.125
- up_weight: bfloat16 [16, 2048, 1024], P('expert', None, 'dp'), may hold values from -0.125 to 0.125
- down_weight: bfloat16 [16, 2048, 1024], P('expert', None, 'dp'), may hold values from -0.1875 to 0.1875
Outputs:
- input_grad: bfloat16 [512, 2048], P('expert', 'dp')
- gate_weight_grad: float32 [16, 2048, 1024], P('expert', None, 'dp')
- up_weight_grad: float32 [16, 2048, 1024], P('expert', None, 'dp')
- down_weight_grad: float32 [16, 2048, 1024], P('expert', None, 'dp')
The draws below stay inside these ranges and needn't reach their ends.
Inputs may be any that keep to these rules, and one draw needn't show every extreme that they name: matching pairs the experts: matching[matching[i]] == i and matching[i] != i. `routes`: each token names 8 different experts; within each aligned block of 32 tokens no expert is named by more than 20 tokens.
All inputs are finite; a program needn't handle non-finite values.
Results may differ from the reference program's by a relative error of at most 0.015.
Values may be sent and summed in bfloat16 or wider, within the bound.
A program may use at most 64 MiB of HBM per device.

```python
import math
import jax
import jax.numpy as jnp
import numpy as np
from jax import lax

D = 2048
HID = 1024
TOPK = 8
TOK_DEV = 32
EXPERTS = 16
CAP = 20
TOKENS = 512
N_DP = 2
N_EXPERT = 16


def draw_matching(key, part):
    order = jax.random.permutation(key, EXPERTS).astype(jnp.int32)
    first = order[0::2]
    second = order[1::2]
    paired = jnp.zeros((EXPERTS,), jnp.int32).at[first].set(second).at[second].set(first)
    return paired.astype(jnp.int32)


def block_scale(stream_key, dims, cuts, low, top_value):
    gain, own = 1.0, jax.random.fold_in(stream_key, 6)
    for position, shards_of in cuts:
        draws = jnp.exp(jax.random.uniform(jax.random.fold_in(own, position), (shards_of,), jnp.float32, low / len(cuts), top_value / len(cuts)))
        gain = gain * jnp.repeat(draws, dims[position] // shards_of).reshape([-1 if axis == position else 1 for axis in range(len(dims))])
    return gain


def assign_block(own_key, own, number, rows, amount, top, most, slope):
    ranking = jax.random.permutation(own_key, amount)
    heavy_load, common = load_shares(amount, rows * top, most, slope, True), load_shares(amount, rows * top, most, slope, False)
    places = jnp.arange(amount)

    def named(sizes, turn):
        used = int((sizes > 0).sum())
        fixed = max(1, used // 4)
        passed = fixed + (places - fixed + turn * (used - fixed)) % max(1, amount - fixed)
        return jnp.zeros((amount,), jnp.int32).at[ranking[jnp.where(places < fixed, places, passed)]].set(jnp.asarray(sizes, jnp.int32))

    sizes = jnp.where(number % 4 == 0, named(heavy_load, number // 4), named(common, number - number // 4 - 1))
    mixed = jax.random.permutation(jax.random.fold_in(own, 3), amount)
    source_of, taker = mixed[0:amount // 2 * 2:2], mixed[1:amount // 2 * 2:2]
    margin = jnp.minimum(sizes[source_of] - 1, most - sizes[taker]) // 2
    margin = jnp.where((source_of == ranking[0]) | (taker == ranking[0]) | (sizes[taker] == 0), 0, jnp.maximum(margin, 0))
    passed = jax.random.randint(jax.random.fold_in(own, 4), (amount // 2,), 0, 1 << 20) % (margin + 1)
    sizes = sizes.at[source_of].add(-passed).at[taker].add(passed)
    labels = jnp.searchsorted(jnp.cumsum(sizes), jnp.arange(rows * top), side="right").astype(jnp.int32)
    grid = labels.reshape(top, rows).T
    grid = grid[jax.random.permutation(jax.random.fold_in(own, 1), rows)]
    turn = jax.random.randint(jax.random.fold_in(own, 2), (rows, 1), 0, top)
    return jnp.take_along_axis(grid, (jnp.arange(top)[None, :] + turn) % top, axis=1)


def load_shares(count, total, most, skew, full):
    portions = [(1 << 20) // math.isqrt(grade ** skew) + 1 for grade in range(1, count + 1)]
    largest = most if full else min(most, max(-(-total // count), total * portions[0] // sum(portions)))
    least = 1 if total - largest >= count - 1 else 0
    holding, spare = [largest] + [least] * (count - 1), total - largest - least * (count - 1)
    while spare > 0:
        free = [i for i in range(1, count) if holding[i] < largest] or [i for i in range(1, count) if holding[i] < most]
        pool, left = sum([portions[i] for i in free]), spare
        for i in free:
            addition = min(most - holding[i], max(1, left * portions[i] // pool), spare)
            holding[i] = holding[i] + addition
            spare = spare - addition
    return np.array(holding)


def normal_values(key, extent, deviation, bound, split=(), kind=jnp.bfloat16):
    drawn = deviation * jax.random.normal(key, extent, jnp.float32)
    if split:
        drawn = drawn * block_scale(key, extent, split, -0.22, 0.18)
    return jnp.clip(drawn, -bound, bound).astype(kind)


def setup_inputs(seed: int = 0) -> dict:
    arg_keys = jax.random.split(jax.random.key(seed), 9)
    tokens = normal_values(arg_keys[0], (TOKENS, D), 1.0, 6.0, ((0, 16), (1, 2)))
    cotangent = normal_values(arg_keys[1], (TOKENS, D), 1.0, 6.0, ((0, 16), (1, 2)))
    routes_keys = jax.random.split(jax.random.fold_in(arg_keys[2], 1), TOKENS // TOK_DEV)
    routes_turns = jax.random.permutation(jax.random.fold_in(arg_keys[2], 3), TOKENS // TOK_DEV)
    routes = jax.vmap(lambda own, number: assign_block(jax.random.fold_in(arg_keys[2], 2), own, number, TOK_DEV, EXPERTS, TOPK, CAP, 2))(routes_keys, routes_turns).reshape((TOKENS, TOPK))
    probs = jnp.clip(jnp.exp(math.log(0.6) - 2.9957323 * jax.random.uniform(arg_keys[3], (TOKENS, TOPK), jnp.float32) ** block_scale(arg_keys[3], (TOKENS, TOPK), ((0, 16),), -0.2, 0.2)), 0.03, 0.6)
    matching = draw_matching(jax.random.fold_in(arg_keys[8], 71), 0)
    gate_weight = normal_values(arg_keys[5], (EXPERTS, D, HID), D ** -0.5, 0.125, ((0, 16), (2, 2)))
    up_weight = normal_values(arg_keys[6], (EXPERTS, D, HID), D ** -0.5, 0.125, ((0, 16), (2, 2)))
    down_weight = normal_values(arg_keys[7], (EXPERTS, D, HID), HID ** -0.5, 0.1875, ((0, 16), (2, 2)))
    return dict(tokens=tokens, cotangent=cotangent, routes=routes, probs=probs, matching=matching, gate_weight=gate_weight, up_weight=up_weight, down_weight=down_weight)


def reference(tokens, cotangent, routes, probs, matching, gate_weight, up_weight, down_weight):
    pair_total = TOKENS * TOPK
    width = N_EXPERT * CAP
    pair_expert = routes.reshape(pair_total).astype(jnp.int32)
    onehot = (pair_expert[:, None] == jnp.arange(EXPERTS, dtype=jnp.int32)[None, :]).astype(jnp.int32)
    running = jnp.cumsum(onehot.reshape(N_EXPERT, TOK_DEV * TOPK, EXPERTS), axis=1).reshape(pair_total, EXPERTS)
    rank = jnp.sum(onehot * running, axis=1) - 1
    source = jnp.arange(pair_total, dtype=jnp.int32) // (TOK_DEV * TOPK)
    slot = (pair_expert * width + source * CAP + rank).astype(jnp.int32)
    index = jnp.full((EXPERTS * width,), pair_total, jnp.int32).at[slot].set(jnp.arange(pair_total, dtype=jnp.int32))
    index = index.reshape(EXPERTS, width)
    pair_in = jnp.concatenate([jnp.repeat(tokens, TOPK, axis=0), jnp.zeros((1, D), jnp.bfloat16)], axis=0)
    scaled = jnp.repeat(cotangent.astype(jnp.float32), TOPK, axis=0) * probs.reshape(pair_total, 1)
    pair_out = jnp.concatenate([scaled.astype(jnp.bfloat16), jnp.zeros((1, D), jnp.bfloat16)], axis=0)
    slice_width = HID // N_DP
    contract_rows = (((0,), (0,)), ((), ()))

    def one_expert(carry, stuff):
        rows, w_gate, w_up, w_down = stuff
        inputs = pair_in[rows]
        grads = pair_out[rows]
        gate = jnp.dot(inputs, w_gate, preferred_element_type=jnp.float32)
        upper = jnp.dot(inputs, w_up, preferred_element_type=jnp.float32)
        sig = jax.nn.sigmoid(gate)
        hidden = (gate * sig * upper).astype(jnp.bfloat16)
        hidden_back = jnp.dot(grads, w_down, preferred_element_type=jnp.float32)
        up_back = (hidden_back * gate * sig).astype(jnp.bfloat16)
        gate_back = (hidden_back * upper * sig * (1.0 + gate * (1.0 - sig))).astype(jnp.bfloat16)
        gate_sum = lax.dot_general(inputs, gate_back, contract_rows, preferred_element_type=jnp.float32)
        up_sum = lax.dot_general(inputs, up_back, contract_rows, preferred_element_type=jnp.float32)
        down_sum = lax.dot_general(grads, hidden, contract_rows, preferred_element_type=jnp.float32)
        gate_slices = gate_back.astype(jnp.float32).reshape(width, N_DP, slice_width)
        up_slices = up_back.astype(jnp.float32).reshape(width, N_DP, slice_width)
        wg_slices = w_gate.astype(jnp.float32).reshape(D, N_DP, slice_width)
        wu_slices = w_up.astype(jnp.float32).reshape(D, N_DP, slice_width)
        slice_part = jnp.einsum("rsh,dsh->rsd", gate_slices, wg_slices) + jnp.einsum("rsh,dsh->rsd", up_slices, wu_slices)
        pair_back = jnp.sum(slice_part.astype(jnp.bfloat16).astype(jnp.float32), axis=1)
        carry = carry.at[rows].add(pair_back)
        return carry, (gate_sum, up_sum, down_sum)

    start = jnp.zeros((pair_total + 1, D), jnp.float32)
    carry, sums = lax.scan(one_expert, start, (index, gate_weight, up_weight, down_weight))
    input_grad = jnp.sum(carry[:pair_total].reshape(TOKENS, TOPK, D), axis=1).astype(jnp.bfloat16)
    gate_sums, up_sums, down_sums = sums
    return (input_grad, jnp.take(gate_sums, matching, axis=0), jnp.take(up_sums, matching, axis=0), jnp.take(down_sums, matching, axis=0))
```

```python
import jax
import jax.numpy as jnp
from jax import lax
from jax.sharding import PartitionSpec as P

contract_rows = (((0,), (0,)), ((), ()))
contract_cols = (((1,), (1,)), ((), ()))


def pair_rows(cotangent, routes, probs, expert):
    weight = jnp.sum(jnp.where(routes == expert, probs, 0.0), axis=1)
    return (cotangent.astype(jnp.float32) * weight[:, None]).astype(jnp.bfloat16)


def local(tokens, cotangent, routes, probs, matching, gate_weight, up_weight, down_weight):
    experts = matching.shape[0]
    tok_rows = routes.shape[0]
    hidden_width = gate_weight.shape[2]
    me = lax.axis_index("expert")
    w_gate, w_up, w_down = gate_weight[0], up_weight[0], down_weight[0]
    routes_all = lax.all_gather(routes, "expert", axis=0, tiled=True)
    probs_all = lax.all_gather(probs, "expert", axis=0, tiled=True)
    both = jnp.stack([tokens, cotangent], axis=0)
    both = lax.all_gather(both, "dp", axis=2, tiled=True)
    both = lax.all_gather(both, "expert", axis=1, tiled=True)
    rows, cot = both[0], both[1]
    grads = pair_rows(cot, routes_all, probs_all, me)
    gate = jnp.dot(rows, w_gate, preferred_element_type=jnp.float32)
    upper = jnp.dot(rows, w_up, preferred_element_type=jnp.float32)
    sig = jax.nn.sigmoid(gate)
    hidden = (gate * sig * upper).astype(jnp.bfloat16)
    hidden_back = jnp.dot(grads, w_down, preferred_element_type=jnp.float32)
    up_back = (hidden_back * gate * sig).astype(jnp.bfloat16)
    gate_back = (hidden_back * upper * sig * (1.0 + gate * (1.0 - sig))).astype(jnp.bfloat16)
    packed = jnp.concatenate([gate_back, up_back, hidden], axis=1)
    packed = packed.reshape(experts, tok_rows, 3 * hidden_width)
    spread = lax.all_to_all(packed, "expert", split_axis=0, concat_axis=0, tiled=True)
    ordered = jnp.take(spread, matching, axis=0)
    landed = lax.all_to_all(ordered, "expert", split_axis=0, concat_axis=0, tiled=True)
    landed = landed.reshape(experts * tok_rows, 3 * hidden_width)
    part = lax.dot_general(gate_back, w_gate, contract_cols, preferred_element_type=jnp.float32)
    part = part + lax.dot_general(up_back, w_up, contract_cols, preferred_element_type=jnp.float32)
    part = part.astype(jnp.bfloat16)
    summed = lax.psum_scatter(part, "dp", scatter_dimension=1, tiled=True)
    summed = summed.reshape(experts, tok_rows, summed.shape[1])
    back = lax.all_to_all(summed, "expert", split_axis=0, concat_axis=0, tiled=True)
    input_grad = jnp.sum(back.astype(jnp.float32), axis=0).astype(jnp.bfloat16)
    partner = matching[me]
    p_grads = pair_rows(cot, routes_all, probs_all, partner)
    g_gate = lax.dot_general(
        rows, landed[:, :hidden_width], contract_rows, preferred_element_type=jnp.float32
    )
    g_up = lax.dot_general(
        rows, landed[:, hidden_width : 2 * hidden_width], contract_rows, preferred_element_type=jnp.float32
    )
    g_down = lax.dot_general(
        p_grads, landed[:, 2 * hidden_width :], contract_rows, preferred_element_type=jnp.float32
    )
    return (
        input_grad,
        g_gate[None],
        g_up[None],
        g_down[None],
    )


def solution(mesh):
    placed = (
        P("expert", "dp"),
        P("expert", "dp"),
        P("expert", None),
        P("expert", None),
        P(),
        P("expert", None, "dp"),
        P("expert", None, "dp"),
        P("expert", None, "dp"),
    )
    return jax.shard_map(
        local,
        mesh=mesh,
        in_specs=placed,
        out_specs=(
            P("expert", "dp"),
            P("expert", None, "dp"),
            P("expert", None, "dp"),
            P("expert", None, "dp"),
        ),
        check_vma=False,
    )
```

```python
import functools

import jax
import jax.numpy as jnp
from jax import lax
from jax.experimental import pallas as pl
from jax.experimental.pallas import tpu as pltpu
from jax.sharding import PartitionSpec as P

contract_rows = (((0,), (0,)), ((), ()))
contract_cols = (((1,), (1,)), ((), ()))
MESH = pl.DeviceIdType.MESH


def bit_count(size):
    return size.bit_length() - 1


def flipped(index, bit):
    step = 2**bit
    return index + step * (1 - 2 * ((index // step) % 2))


def gather_orders(expert_bits, dp_bits):
    far = [("expert", b) for b in range(expert_bits - 1, 1, -1)]
    mid = [("expert", 1)]
    last = [("expert", 0)]
    across = [("dp", b) for b in range(dp_bits)]
    return (far + across + mid + last, far + mid + across + last, far + mid + last)


def gather_kernel(
    n_expert, n_dp, tokens, cotangent, table, all_tokens, all_cotangent, all_table, send, recv, own
):
    e = lax.axis_index("expert")
    d = lax.axis_index("dp")
    expert_bits, dp_bits = bit_count(n_expert), bit_count(n_dp)
    width = tokens.shape[1]
    half = tokens.shape[0] // 2

    def peer(axis, bit):
        if axis == "expert":
            return (d, flipped(e, bit))
        return (flipped(d, bit), e)

    def held(ref, done, rows, data):
        where = []
        for b in range(expert_bits - 1, -1, -1):
            where.append(slice(None) if ("expert", b) in done else (e // 2**b) % 2)
        where.append(rows)
        if data:
            k = len([x for x in done if x[0] == "dp"])
            start = pl.multiple_of((d // 2**k) * (2**k * width), width)
            where.append(pl.ds(start, 2**k * width))
        else:
            where.append(slice(None))
        return ref.at[tuple(where)]

    barrier = pltpu.get_barrier_semaphore()
    links = [("expert", b) for b in range(expert_bits)] + [("dp", b) for b in range(dp_bits)]
    for link in links:
        pl.semaphore_signal(barrier, inc=1, device_id=peer(*link), device_id_type=MESH)

    first, second, plain = gather_orders(expert_bits, dp_bits)
    top, low, whole = pl.ds(0, half), pl.ds(half, half), pl.ds(0, 2 * half)
    parts = [
        (tokens, all_tokens, top, first, True),
        (tokens, all_tokens, low, second, True),
        (cotangent, all_cotangent, top, first, True),
        (cotangent, all_cotangent, low, second, True),
        (table, all_table, whole, plain, False),
    ]
    locals_ = []
    for i, (src, dst, rows, order, data) in enumerate(parts):
        c = pltpu.make_async_copy(src.at[rows], held(dst, [], rows, data), own.at[i])
        c.start()
        locals_.append(c)
    pl.semaphore_wait(barrier, len(links))
    flights = [[] for _ in parts]
    steps = max(len(p[3]) for p in parts)
    for s in range(steps):
        for i, (src, dst, rows, order, data) in enumerate(parts):
            if s >= len(order):
                continue
            if s == 0:
                locals_[i].wait()
            else:
                flights[i][s - 1].wait_recv()
            block = held(dst, order[:s], rows, data)
            c = pltpu.make_async_remote_copy(
                src_ref=block,
                dst_ref=block,
                send_sem=send.at[i, s],
                recv_sem=recv.at[i, s],
                device_id=peer(*order[s]),
                device_id_type=MESH,
            )
            c.start()
            flights[i].append(c)
    for f in flights:
        f[-1].wait_recv()
        for c in f:
            c.wait_send()


def gather_all(n_expert, n_dp, tokens, cotangent, table):
    lead = (2,) * bit_count(n_expert)
    rows, width = tokens.shape
    steps = bit_count(n_expert) + bit_count(n_dp)
    wide = jax.ShapeDtypeStruct(lead + (rows, width * n_dp), tokens.dtype)
    small = jax.ShapeDtypeStruct(lead + table.shape, table.dtype)
    outs = pl.pallas_call(
        functools.partial(gather_kernel, n_expert, n_dp),
        out_shape=(wide, wide, small),
        in_specs=[pl.BlockSpec(memory_space=pltpu.VMEM)] * 3,
        out_specs=[pl.BlockSpec(memory_space=pl.ANY)] * 3,
        scratch_shapes=[
            pltpu.SemaphoreType.DMA((5, steps)),
            pltpu.SemaphoreType.DMA((5, steps)),
            pltpu.SemaphoreType.DMA((5,)),
        ],
        compiler_params=pltpu.CompilerParams(collective_id=0, has_side_effects=True),
    )(tokens, cotangent, table)
    total = n_expert * rows
    return (
        outs[0].reshape(total, width * n_dp),
        outs[1].reshape(total, width * n_dp),
        outs[2].reshape(total, table.shape[1]),
    )


def column(table, index):
    lanes = lax.broadcasted_iota(jnp.int32, table.shape, 1)
    return jnp.sum(jnp.where(lanes == index, table, 0.0), axis=1)


def scaled(cotangent, weight):
    return (cotangent.astype(jnp.float32) * weight[:, None]).astype(jnp.bfloat16)


def selector(weight, blocks, capacity, kinds, slots):
    chosen = (weight > 0.0).reshape(blocks, -1)
    tok_rows = chosen.shape[1]
    at = lax.broadcasted_iota(jnp.int32, (tok_rows, tok_rows), 0)
    to = lax.broadcasted_iota(jnp.int32, (tok_rows, tok_rows), 1)
    upto = jnp.where(at <= to, 1.0, 0.0).astype(jnp.bfloat16)
    rank = jnp.dot(chosen.astype(jnp.bfloat16), upto, preferred_element_type=jnp.float32)
    rank = jnp.where(chosen, rank.astype(jnp.int32) - 1, -1)
    wide = jnp.concatenate([rank] * kinds, axis=1)[:, None, :]
    shape = (blocks, slots, kinds * tok_rows)
    slot = lax.broadcasted_iota(jnp.int32, shape, 1)
    kind = lax.broadcasted_iota(jnp.int32, shape, 2) // tok_rows
    hit = (wide >= 0) & (wide + kind * capacity == slot)
    return jnp.where(hit, 1.0, 0.0).astype(jnp.bfloat16)


def local(n_expert, n_dp, tokens, cotangent, routes, probs, matching, w_gate, w_up, w_down):
    experts = matching.shape[0]
    tok_rows, top_count = routes.shape
    w_gate, w_up, w_down = w_gate[0], w_up[0], w_down[0]
    hidden_width = w_gate.shape[1]
    capacity = max(2, 5 * tok_rows * top_count // (4 * experts))
    slots = -(-3 * capacity // 16) * 16
    me = lax.axis_index("expert")
    lanes = -(-experts // 128) * 128
    names = jnp.arange(lanes, dtype=jnp.int32)
    table = jnp.sum(
        jnp.where(routes[:, :, None] == names[None, None, :], probs[:, :, None], 0.0), axis=1
    )
    rows, cot, table = gather_all(n_expert, n_dp, tokens, cotangent, table)
    weight = column(table, me)
    grads = scaled(cot, weight)
    gate = jnp.dot(rows, w_gate, preferred_element_type=jnp.float32)
    upper = jnp.dot(rows, w_up, preferred_element_type=jnp.float32)
    sig = jax.nn.sigmoid(gate)
    hidden = (gate * sig * upper).astype(jnp.bfloat16)
    hidden_back = jnp.dot(grads, w_down, preferred_element_type=jnp.float32)
    up_back = (hidden_back * gate * sig).astype(jnp.bfloat16)
    gate_back = (hidden_back * upper * sig * (1.0 + gate * (1.0 - sig))).astype(jnp.bfloat16)
    cubes = [v.reshape(experts, tok_rows, hidden_width) for v in (gate_back, up_back, hidden)]
    stacked = jnp.concatenate(cubes, axis=1)
    pick = selector(weight, experts, capacity, 3, slots)
    packed = jnp.einsum(
        "jrt,jth->jrh", pick, stacked, preferred_element_type=jnp.float32
    ).astype(jnp.bfloat16)
    spread = lax.all_to_all(packed, "expert", split_axis=0, concat_axis=0, tiled=True)
    ordered = jnp.take(spread, matching, axis=0)
    landed = lax.all_to_all(ordered, "expert", split_axis=0, concat_axis=0, tiled=True)
    part = lax.dot_general(gate_back, w_gate, contract_cols, preferred_element_type=jnp.float32)
    part = part + lax.dot_general(up_back, w_up, contract_cols, preferred_element_type=jnp.float32)
    part = part.astype(jnp.bfloat16)
    summed = lax.psum_scatter(part, "dp", scatter_dimension=1, tiled=True)
    summed = summed.reshape(experts, tok_rows, summed.shape[1])
    back = lax.all_to_all(summed, "expert", split_axis=0, concat_axis=0, tiled=True)
    input_grad = jnp.sum(back.astype(jnp.float32), axis=0).astype(jnp.bfloat16)
    p_weight = column(table, matching[me])
    p_pick = selector(p_weight, experts, capacity, 3, slots)
    dense = jnp.einsum(
        "jrt,jrh->jth", p_pick, landed, preferred_element_type=jnp.float32
    ).astype(jnp.bfloat16)
    p_grads = scaled(cot, p_weight)
    total = experts * tok_rows

    def take(kind):
        return dense[:, kind * tok_rows : (kind + 1) * tok_rows].reshape(total, hidden_width)

    g_gate = lax.dot_general(rows, take(0), contract_rows, preferred_element_type=jnp.float32)
    g_up = lax.dot_general(rows, take(1), contract_rows, preferred_element_type=jnp.float32)
    g_down = lax.dot_general(p_grads, take(2), contract_rows, preferred_element_type=jnp.float32)
    return (input_grad, g_gate[None], g_up[None], g_down[None])


def solution(mesh):
    weights = P("expert", None, "dp")
    return jax.shard_map(
        functools.partial(local, mesh.shape["expert"], mesh.shape["dp"]),
        mesh=mesh,
        in_specs=(
            P("expert", "dp"),
            P("expert", "dp"),
            P("expert", None),
            P("expert", None),
            P(),
            weights,
            weights,
            weights,
        ),
        out_specs=(P("expert", "dp"), weights, weights, weights),
        check_vma=False,
    )
```

```python
import functools

import jax
import jax.numpy as jnp
from jax import lax
from jax.experimental import pallas as pl
from jax.experimental.pallas import tpu as pltpu
from jax.sharding import PartitionSpec as P

contract_rows = (((0,), (0,)), ((), ()))
contract_cols = (((1,), (1,)), ((), ()))
MESH = pl.DeviceIdType.MESH


def bit_count(size):
    return size.bit_length() - 1


def flipped(index, bit):
    step = 2**bit
    return index + step * (1 - 2 * ((index // step) % 2))


def gather_orders(expert_bits, dp_bits):
    far = [("expert", b) for b in range(expert_bits - 1, 1, -1)]
    mid = [("expert", 1)]
    last = [("expert", 0)]
    across = [("dp", b) for b in range(dp_bits)]
    return (far + across + mid + last, far + mid + across + last, far + mid + last)


def gather_kernel(
    n_expert, n_dp, tokens, cotangent, table, all_tokens, all_cotangent, all_table, send, recv, own
):
    e = lax.axis_index("expert")
    d = lax.axis_index("dp")
    expert_bits, dp_bits = bit_count(n_expert), bit_count(n_dp)
    width = tokens.shape[1]
    half = tokens.shape[0] // 2

    def peer(axis, bit):
        if axis == "expert":
            return (d, flipped(e, bit))
        return (flipped(d, bit), e)

    def held(ref, done, rows, data):
        where = []
        for b in range(expert_bits - 1, -1, -1):
            where.append(slice(None) if ("expert", b) in done else (e // 2**b) % 2)
        where.append(rows)
        if data:
            k = len([x for x in done if x[0] == "dp"])
            start = pl.multiple_of((d // 2**k) * (2**k * width), width)
            where.append(pl.ds(start, 2**k * width))
        else:
            where.append(slice(None))
        return ref.at[tuple(where)]

    barrier = pltpu.get_barrier_semaphore()
    links = [("expert", b) for b in range(expert_bits)] + [("dp", b) for b in range(dp_bits)]
    for link in links:
        pl.semaphore_signal(barrier, inc=1, device_id=peer(*link), device_id_type=MESH)

    first, second, plain = gather_orders(expert_bits, dp_bits)
    top, low, whole = pl.ds(0, half), pl.ds(half, half), pl.ds(0, 2 * half)
    parts = [
        (tokens, all_tokens, top, first, True),
        (tokens, all_tokens, low, second, True),
        (cotangent, all_cotangent, top, first, True),
        (cotangent, all_cotangent, low, second, True),
        (table, all_table, whole, plain, False),
    ]
    locals_ = []
    for i, (src, dst, rows, order, data) in enumerate(parts):
        c = pltpu.make_async_copy(src.at[rows], held(dst, [], rows, data), own.at[i])
        c.start()
        locals_.append(c)
    pl.semaphore_wait(barrier, len(links))
    flights = [[] for _ in parts]
    steps = max(len(p[3]) for p in parts)
    for s in range(steps):
        for i, (src, dst, rows, order, data) in enumerate(parts):
            if s >= len(order):
                continue
            if s == 0:
                locals_[i].wait()
            else:
                flights[i][s - 1].wait_recv()
            block = held(dst, order[:s], rows, data)
            c = pltpu.make_async_remote_copy(
                src_ref=block,
                dst_ref=block,
                send_sem=send.at[i, s],
                recv_sem=recv.at[i, s],
                device_id=peer(*order[s]),
                device_id_type=MESH,
            )
            c.start()
            flights[i].append(c)
    for f in flights:
        f[-1].wait_recv()
        for c in f:
            c.wait_send()


def gather_all(n_expert, n_dp, tokens, cotangent, table):
    lead = (2,) * bit_count(n_expert)
    rows, width = tokens.shape
    steps = bit_count(n_expert) + bit_count(n_dp)
    wide = jax.ShapeDtypeStruct(lead + (rows, width * n_dp), tokens.dtype)
    small = jax.ShapeDtypeStruct(lead + table.shape, table.dtype)
    outs = pl.pallas_call(
        functools.partial(gather_kernel, n_expert, n_dp),
        out_shape=(wide, wide, small),
        in_specs=[pl.BlockSpec(memory_space=pltpu.VMEM)] * 3,
        out_specs=[pl.BlockSpec(memory_space=pl.ANY)] * 3,
        scratch_shapes=[
            pltpu.SemaphoreType.DMA((5, steps)),
            pltpu.SemaphoreType.DMA((5, steps)),
            pltpu.SemaphoreType.DMA((5,)),
        ],
        compiler_params=pltpu.CompilerParams(collective_id=0, has_side_effects=True),
    )(tokens, cotangent, table)
    total = n_expert * rows
    return (
        outs[0].reshape(total, width * n_dp),
        outs[1].reshape(total, width * n_dp),
        outs[2].reshape(total, table.shape[1]),
    )


def reduce_orders(expert_bits, dp_bits):
    far = [("expert", b) for b in range(2, expert_bits)]
    mid = [("expert", 1)]
    near = [("expert", 0)]
    across = [("dp", b) for b in range(dp_bits - 1, -1, -1)]
    return (near + across + mid + far, near + mid + across + far)


def reduce_shapes(order, expert_bits, dp_bits, rows, width):
    left_e, left_d = expert_bits, dp_bits
    shapes = []
    for axis, _ in order:
        if axis == "expert":
            left_e -= 1
        else:
            left_d -= 1
        shapes.append((2,) * left_e + (rows, width * 2**left_d))
    return shapes


def exchange_kernel(n_expert, n_dp, chunks, match, packed, part, landed, result, *scratch):
    e = lax.axis_index("expert")
    d = lax.axis_index("dp")
    expert_bits, dp_bits = bit_count(n_expert), bit_count(n_dp)
    steps = expert_bits + dp_bits
    halves = 2
    sums = [scratch[i * steps : (i + 1) * steps] for i in range(halves)]
    came = [scratch[(halves + i) * steps : (halves + i + 1) * steps] for i in range(halves)]
    rest = scratch[2 * halves * steps :]
    arrived = rest[:chunks]
    ordered, send1, recv1, send2, recv2, own, rsend, rrecv = rest[chunks:]
    size = packed.shape[1] // chunks
    width = result.shape[1]
    half = result.shape[0] // halves

    def peer(axis, bit):
        if axis == "expert":
            return (d, flipped(e, bit))
        return (flipped(d, bit), e)

    barrier = pltpu.get_barrier_semaphore()

    @pl.loop(1, n_expert)
    def _(o):
        pl.semaphore_signal(barrier, inc=1, device_id=(d, (e + o) % n_expert), device_id_type=MESH)

    for b in range(dp_bits):
        pl.semaphore_signal(barrier, inc=1, device_id=(flipped(d, b), e), device_id_type=MESH)

    def rows_of(c):
        return pl.ds(c * size, size)

    stay = [
        pltpu.make_async_copy(packed.at[e, rows_of(c)], arrived[c].at[e], own.at[0, c])
        for c in range(chunks)
    ]
    for c in stay:
        c.start()
    pl.semaphore_wait(barrier, n_expert - 1 + dp_bits)

    def first(c, o):
        to = (e + o) % n_expert
        return pltpu.make_async_remote_copy(
            src_ref=packed.at[to, rows_of(c)],
            dst_ref=arrived[c].at[e],
            send_sem=send1.at[c, o],
            recv_sem=recv1.at[c, o],
            device_id=(d, to),
            device_id_type=MESH,
        )

    def second(c, o):
        return pltpu.make_async_remote_copy(
            src_ref=ordered.at[o, rows_of(c)],
            dst_ref=landed.at[e, rows_of(c)],
            send_sem=send2.at[c, o],
            recv_sem=recv2.at[c, o],
            device_id=(d, (e + o) % n_expert),
            device_id_type=MESH,
        )

    orders = reduce_orders(expert_bits, dp_bits)
    flights = [[], []]

    def split(i, s):
        axis, bit = orders[i][s]
        if s == 0:
            ref, rows = part, pl.ds(i * half, half)
        else:
            ref, rows = sums[i][s - 1], slice(None)
        left = [b for a, b in orders[i][s:] if a == "expert"]
        left = sorted(left, reverse=True)
        if axis == "expert":
            mine = (e // 2**bit) % 2
            at = left.index(bit)

            def where(v):
                return tuple([slice(None)] * at + [v] + [slice(None)] * (len(left) - at - 1)) + (
                    rows,
                    slice(None),
                )

            return ref, where(mine), where(1 - mine)
        mine = (d // 2**bit) % 2
        span = 2**bit * width
        head = (slice(None),) * len(left) + (rows,)
        keep = head + (pl.ds(pl.multiple_of(mine * span, 128), span),)
        give = head + (pl.ds(pl.multiple_of((1 - mine) * span, 128), span),)
        return ref, keep, give

    def start_step(i, s):
        ref, _, give = split(i, s)
        c = pltpu.make_async_remote_copy(
            src_ref=ref.at[give],
            dst_ref=came[i][s],
            send_sem=rsend.at[i, s],
            recv_sem=rrecv.at[i, s],
            device_id=peer(*orders[i][s]),
            device_id_type=MESH,
        )
        c.start()
        flights[i].append(c)

    def end_step(i, s):
        ref, keep, _ = split(i, s)
        flights[i][s].wait_recv()
        total = ref[keep].astype(jnp.float32) + came[i][s][...].astype(jnp.float32)
        sums[i][s][...] = total.astype(sums[i][s].dtype)

    for i in range(halves):
        start_step(i, 0)
    for c in range(chunks):

        @pl.loop(1, n_expert)
        def _(o):
            first(c, o).start()

    early = min(2, steps - 1)
    for s in range(early):
        for i in range(halves):
            end_step(i, s)
            start_step(i, s + 1)
    for c in range(chunks):
        stay[c].wait()

        @pl.loop(1, n_expert)
        def _(o):
            first(c, o).wait_recv()

        @pl.loop(0, n_expert)
        def _(o):
            source = match[(e + o) % n_expert]
            ordered[o, rows_of(c), :] = arrived[c][source]

        pltpu.make_async_copy(
            ordered.at[0, rows_of(c)], landed.at[e, rows_of(c)], own.at[1, c]
        ).start()

        @pl.loop(1, n_expert)
        def _(o):
            second(c, o).start()

    for s in range(early, steps):
        for i in range(halves):
            end_step(i, s)
            if s + 1 < steps:
                start_step(i, s + 1)
    for i in range(halves):
        result[pl.ds(i * half, half), :] = sums[i][steps - 1][...]
    for c in range(chunks):
        pltpu.make_async_copy(
            ordered.at[0, rows_of(c)], landed.at[e, rows_of(c)], own.at[1, c]
        ).wait()

        @pl.loop(1, n_expert)
        def _(o):
            second(c, o).wait_recv()
            first(c, o).wait_send()
            second(c, o).wait_send()

    for f in flights:
        for c in f:
            c.wait_send()


def exchange(n_expert, n_dp, matching, packed, part, tok_rows, width):
    expert_bits, dp_bits = bit_count(n_expert), bit_count(n_dp)
    steps = expert_bits + dp_bits
    chunks = 2 if packed.shape[1] % 32 == 0 else 1
    buffers = []
    for order in reduce_orders(expert_bits, dp_bits):
        for shape in reduce_shapes(order, expert_bits, dp_bits, tok_rows // 2, width):
            buffers.append(pltpu.VMEM(shape, part.dtype))
    return pl.pallas_call(
        functools.partial(exchange_kernel, n_expert, n_dp, chunks),
        out_shape=(
            jax.ShapeDtypeStruct(packed.shape, packed.dtype),
            jax.ShapeDtypeStruct((tok_rows, width), part.dtype),
        ),
        in_specs=[
            pl.BlockSpec(memory_space=pltpu.SMEM),
            pl.BlockSpec(memory_space=pltpu.VMEM),
            pl.BlockSpec(memory_space=pltpu.VMEM),
        ],
        out_specs=[pl.BlockSpec(memory_space=pltpu.VMEM)] * 2,
        scratch_shapes=buffers
        + buffers
        + [pltpu.VMEM((n_expert, packed.shape[1] // chunks, packed.shape[2]), packed.dtype)] * chunks
        + [
            pltpu.VMEM(packed.shape, packed.dtype),
            pltpu.SemaphoreType.DMA((chunks, n_expert)),
            pltpu.SemaphoreType.DMA((chunks, n_expert)),
            pltpu.SemaphoreType.DMA((chunks, n_expert)),
            pltpu.SemaphoreType.DMA((chunks, n_expert)),
            pltpu.SemaphoreType.DMA((2, chunks)),
            pltpu.SemaphoreType.DMA((2, steps)),
            pltpu.SemaphoreType.DMA((2, steps)),
        ],
        compiler_params=pltpu.CompilerParams(collective_id=1, has_side_effects=True),
    )(matching, packed, part.reshape((2,) * expert_bits + (tok_rows, part.shape[1])))


def column(table, index):
    lanes = lax.broadcasted_iota(jnp.int32, table.shape, 1)
    return jnp.sum(jnp.where(lanes == index, table, 0.0), axis=1)


def scaled(cotangent, weight):
    return (cotangent.astype(jnp.float32) * weight[:, None]).astype(jnp.bfloat16)


def selector(weight, blocks, capacity, kinds, slots):
    chosen = (weight > 0.0).reshape(blocks, -1)
    tok_rows = chosen.shape[1]
    at = lax.broadcasted_iota(jnp.int32, (tok_rows, tok_rows), 0)
    to = lax.broadcasted_iota(jnp.int32, (tok_rows, tok_rows), 1)
    upto = jnp.where(at <= to, 1.0, 0.0).astype(jnp.bfloat16)
    rank = jnp.dot(chosen.astype(jnp.bfloat16), upto, preferred_element_type=jnp.float32)
    rank = jnp.where(chosen, rank.astype(jnp.int32) - 1, -1)
    wide = jnp.concatenate([rank] * kinds, axis=1)[:, None, :]
    shape = (blocks, slots, kinds * tok_rows)
    slot = lax.broadcasted_iota(jnp.int32, shape, 1)
    kind = lax.broadcasted_iota(jnp.int32, shape, 2) // tok_rows
    hit = (wide >= 0) & (wide + kind * capacity == slot)
    return jnp.where(hit, 1.0, 0.0).astype(jnp.bfloat16)


def local(n_expert, n_dp, tokens, cotangent, routes, probs, matching, w_gate, w_up, w_down):
    experts = matching.shape[0]
    tok_rows, top_count = routes.shape
    w_gate, w_up, w_down = w_gate[0], w_up[0], w_down[0]
    hidden_width = w_gate.shape[1]
    capacity = max(2, 5 * tok_rows * top_count // (4 * experts))
    slots = -(-3 * capacity // 16) * 16
    me = lax.axis_index("expert")
    lanes = -(-experts // 128) * 128
    names = jnp.arange(lanes, dtype=jnp.int32)
    table = jnp.sum(
        jnp.where(routes[:, :, None] == names[None, None, :], probs[:, :, None], 0.0), axis=1
    )
    rows, cot, table = gather_all(n_expert, n_dp, tokens, cotangent, table)
    weight = column(table, me)
    grads = scaled(cot, weight)
    gate = jnp.dot(rows, w_gate, preferred_element_type=jnp.float32)
    upper = jnp.dot(rows, w_up, preferred_element_type=jnp.float32)
    sig = jax.nn.sigmoid(gate)
    hidden = (gate * sig * upper).astype(jnp.bfloat16)
    hidden_back = jnp.dot(grads, w_down, preferred_element_type=jnp.float32)
    up_back = (hidden_back * gate * sig).astype(jnp.bfloat16)
    gate_back = (hidden_back * upper * sig * (1.0 + gate * (1.0 - sig))).astype(jnp.bfloat16)
    cubes = [v.reshape(experts, tok_rows, hidden_width) for v in (gate_back, up_back, hidden)]
    stacked = jnp.concatenate(cubes, axis=1)
    pick = selector(weight, experts, capacity, 3, slots)
    packed = jnp.einsum(
        "jrt,jth->jrh", pick, stacked, preferred_element_type=jnp.float32
    ).astype(jnp.bfloat16)
    part = lax.dot_general(gate_back, w_gate, contract_cols, preferred_element_type=jnp.float32)
    part = part + lax.dot_general(up_back, w_up, contract_cols, preferred_element_type=jnp.float32)
    part = part.astype(jnp.bfloat16)
    landed, input_grad = exchange(
        n_expert, n_dp, matching, packed, part, tok_rows, tokens.shape[1]
    )
    p_weight = column(table, matching[me])
    p_pick = selector(p_weight, experts, capacity, 3, slots)
    dense = jnp.einsum(
        "jrt,jrh->jth", p_pick, landed, preferred_element_type=jnp.float32
    ).astype(jnp.bfloat16)
    p_grads = scaled(cot, p_weight)
    total = experts * tok_rows

    def take(kind):
        return dense[:, kind * tok_rows : (kind + 1) * tok_rows].reshape(total, hidden_width)

    g_gate = lax.dot_general(rows, take(0), contract_rows, preferred_element_type=jnp.float32)
    g_up = lax.dot_general(rows, take(1), contract_rows, preferred_element_type=jnp.float32)
    g_down = lax.dot_general(p_grads, take(2), contract_rows, preferred_element_type=jnp.float32)
    return (input_grad, g_gate[None], g_up[None], g_down[None])


def solution(mesh):
    weights = P("expert", None, "dp")
    return jax.shard_map(
        functools.partial(local, mesh.shape["expert"], mesh.shape["dp"]),
        mesh=mesh,
        in_specs=(
            P("expert", "dp"),
            P("expert", "dp"),
            P("expert", None),
            P("expert", None),
            P(),
            weights,
            weights,
            weights,
        ),
        out_specs=(P("expert", "dp"), weights, weights, weights),
        check_vma=False,
    )
```

```python
import functools

import jax
import jax.numpy as jnp
from jax import lax
from jax.experimental import pallas as pl
from jax.experimental.pallas import tpu as pltpu
from jax.sharding import PartitionSpec as P

contract_rows = (((0,), (0,)), ((), ()))
contract_cols = (((1,), (1,)), ((), ()))
MESH = pl.DeviceIdType.MESH


def bit_count(size):
    return size.bit_length() - 1


def flipped(index, bit):
    step = 2**bit
    return index + step * (1 - 2 * ((index // step) % 2))


def gather_orders(expert_bits, dp_bits):
    far = [("expert", b) for b in range(expert_bits - 1, 1, -1)]
    mid = [("expert", 1)]
    last = [("expert", 0)]
    across = [("dp", b) for b in range(dp_bits)]
    return (
        far + across + mid + last,
        far + mid + across + last,
        across + far + mid + last,
        mid + far + across + last,
        far + mid + last,
    )


def gather_kernel(
    n_expert, n_dp, tokens, cotangent, table, all_tokens, all_cotangent, all_table, send, recv, own
):
    e = lax.axis_index("expert")
    d = lax.axis_index("dp")
    expert_bits, dp_bits = bit_count(n_expert), bit_count(n_dp)
    width = tokens.shape[1]
    half = tokens.shape[0] // 2

    def peer(axis, bit):
        if axis == "expert":
            return (d, flipped(e, bit))
        return (flipped(d, bit), e)

    def held(ref, done, rows, data):
        where = []
        for b in range(expert_bits - 1, -1, -1):
            where.append(slice(None) if ("expert", b) in done else (e // 2**b) % 2)
        where.append(rows)
        if data:
            k = len([x for x in done if x[0] == "dp"])
            start = pl.multiple_of((d // 2**k) * (2**k * width), width)
            where.append(pl.ds(start, 2**k * width))
        else:
            where.append(slice(None))
        return ref.at[tuple(where)]

    barrier = pltpu.get_barrier_semaphore()
    links = [("expert", b) for b in range(expert_bits)] + [("dp", b) for b in range(dp_bits)]
    for link in links:
        pl.semaphore_signal(barrier, inc=1, device_id=peer(*link), device_id_type=MESH)

    orders = gather_orders(expert_bits, dp_bits)
    top, low, whole = pl.ds(0, half), pl.ds(half, half), pl.ds(0, 2 * half)
    parts = [
        (tokens, all_tokens, top, orders[0], True),
        (tokens, all_tokens, low, orders[2], True),
        (cotangent, all_cotangent, top, orders[1], True),
        (cotangent, all_cotangent, low, orders[3], True),
        (table, all_table, whole, orders[4], False),
    ]
    locals_ = []
    for i, (src, dst, rows, order, data) in enumerate(parts):
        c = pltpu.make_async_copy(src.at[rows], held(dst, [], rows, data), own.at[i])
        c.start()
        locals_.append(c)
    pl.semaphore_wait(barrier, len(links))
    flights = [[] for _ in parts]
    steps = max(len(p[3]) for p in parts)
    for s in range(steps):
        turn = (4, 1, 3, 0, 2) if s < 2 else (4, 0, 2, 1, 3)
        for i in turn:
            src, dst, rows, order, data = parts[i]
            if s >= len(order):
                continue
            if s == 0:
                locals_[i].wait()
            else:
                flights[i][s - 1].wait_recv()
            block = held(dst, order[:s], rows, data)
            c = pltpu.make_async_remote_copy(
                src_ref=block,
                dst_ref=block,
                send_sem=send.at[i, s],
                recv_sem=recv.at[i, s],
                device_id=peer(*order[s]),
                device_id_type=MESH,
            )
            c.start()
            flights[i].append(c)
    for f in flights:
        f[-1].wait_recv()
        for c in f:
            c.wait_send()


def gather_all(n_expert, n_dp, tokens, cotangent, table):
    lead = (2,) * bit_count(n_expert)
    rows, width = tokens.shape
    steps = bit_count(n_expert) + bit_count(n_dp)
    wide = jax.ShapeDtypeStruct(lead + (rows, width * n_dp), tokens.dtype)
    small = jax.ShapeDtypeStruct(lead + table.shape, table.dtype)
    outs = pl.pallas_call(
        functools.partial(gather_kernel, n_expert, n_dp),
        out_shape=(wide, wide, small),
        in_specs=[pl.BlockSpec(memory_space=pltpu.VMEM)] * 3,
        out_specs=[pl.BlockSpec(memory_space=pl.ANY)] * 3,
        scratch_shapes=[
            pltpu.SemaphoreType.DMA((5, steps)),
            pltpu.SemaphoreType.DMA((5, steps)),
            pltpu.SemaphoreType.DMA((5,)),
        ],
        compiler_params=pltpu.CompilerParams(collective_id=0, has_side_effects=True),
    )(tokens, cotangent, table)
    total = n_expert * rows
    return (
        outs[0].reshape(total, width * n_dp),
        outs[1].reshape(total, width * n_dp),
        outs[2].reshape(total, table.shape[1]),
    )


def reduce_orders(expert_bits, dp_bits):
    far = [("expert", b) for b in range(2, expert_bits)]
    mid = [("expert", 1)]
    near = [("expert", 0)]
    across = [("dp", b) for b in range(dp_bits - 1, -1, -1)]
    return (near + across + mid + far, near + mid + across + far)


def reduce_shapes(order, expert_bits, dp_bits, rows, width):
    left_e, left_d = expert_bits, dp_bits
    shapes = []
    for axis, _ in order:
        if axis == "expert":
            left_e -= 1
        else:
            left_d -= 1
        shapes.append((2,) * left_e + (rows, width * 2**left_d))
    return shapes


def exchange_kernel(n_expert, n_dp, chunks, match, packed, part, landed, result, *scratch):
    e = lax.axis_index("expert")
    d = lax.axis_index("dp")
    expert_bits, dp_bits = bit_count(n_expert), bit_count(n_dp)
    steps = expert_bits + dp_bits
    halves = 2
    sums = [scratch[i * steps : (i + 1) * steps] for i in range(halves)]
    came = [scratch[(halves + i) * steps : (halves + i + 1) * steps] for i in range(halves)]
    rest = scratch[2 * halves * steps :]
    arrived = rest[:chunks]
    ordered, send1, recv1, send2, recv2, own, rsend, rrecv = rest[chunks:]
    size = packed.shape[1] // chunks
    width = result.shape[1]
    half = result.shape[0] // halves

    def peer(axis, bit):
        if axis == "expert":
            return (d, flipped(e, bit))
        return (flipped(d, bit), e)

    barrier = pltpu.get_barrier_semaphore()

    @pl.loop(1, n_expert)
    def _(o):
        pl.semaphore_signal(barrier, inc=1, device_id=(d, (e + o) % n_expert), device_id_type=MESH)

    for b in range(dp_bits):
        pl.semaphore_signal(barrier, inc=1, device_id=(flipped(d, b), e), device_id_type=MESH)

    def rows_of(c):
        return pl.ds(c * size, size)

    stay = [
        pltpu.make_async_copy(packed.at[e, rows_of(c)], arrived[c].at[e], own.at[0, c])
        for c in range(chunks)
    ]
    for c in stay:
        c.start()
    pl.semaphore_wait(barrier, n_expert - 1 + dp_bits)

    def first(c, o):
        to = (e + o) % n_expert
        return pltpu.make_async_remote_copy(
            src_ref=packed.at[to, rows_of(c)],
            dst_ref=arrived[c].at[e],
            send_sem=send1.at[c, o],
            recv_sem=recv1.at[c, o],
            device_id=(d, to),
            device_id_type=MESH,
        )

    def second(c, o):
        return pltpu.make_async_remote_copy(
            src_ref=ordered.at[o, rows_of(c)],
            dst_ref=landed.at[e, rows_of(c)],
            send_sem=send2.at[c, o],
            recv_sem=recv2.at[c, o],
            device_id=(d, (e + o) % n_expert),
            device_id_type=MESH,
        )

    orders = reduce_orders(expert_bits, dp_bits)
    flights = [[], []]

    def split(i, s):
        axis, bit = orders[i][s]
        if s == 0:
            ref, rows = part, pl.ds(i * half, half)
        else:
            ref, rows = sums[i][s - 1], slice(None)
        left = [b for a, b in orders[i][s:] if a == "expert"]
        left = sorted(left, reverse=True)
        if axis == "expert":
            mine = (e // 2**bit) % 2
            at = left.index(bit)

            def where(v):
                return tuple([slice(None)] * at + [v] + [slice(None)] * (len(left) - at - 1)) + (
                    rows,
                    slice(None),
                )

            return ref, where(mine), where(1 - mine)
        mine = (d // 2**bit) % 2
        span = 2**bit * width
        head = (slice(None),) * len(left) + (rows,)
        keep = head + (pl.ds(pl.multiple_of(mine * span, 128), span),)
        give = head + (pl.ds(pl.multiple_of((1 - mine) * span, 128), span),)
        return ref, keep, give

    def start_step(i, s):
        ref, _, give = split(i, s)
        c = pltpu.make_async_remote_copy(
            src_ref=ref.at[give],
            dst_ref=came[i][s],
            send_sem=rsend.at[i, s],
            recv_sem=rrecv.at[i, s],
            device_id=peer(*orders[i][s]),
            device_id_type=MESH,
        )
        c.start()
        flights[i].append(c)

    def end_step(i, s):
        ref, keep, _ = split(i, s)
        flights[i][s].wait_recv()
        total = ref[keep].astype(jnp.float32) + came[i][s][...].astype(jnp.float32)
        sums[i][s][...] = total.astype(sums[i][s].dtype)

    for i in range(halves):
        start_step(i, 0)
    for c in range(chunks):

        @pl.loop(1, n_expert)
        def _(o):
            first(c, o).start()

    early = min(2, steps - 1)
    for s in range(early):
        for i in range(halves):
            end_step(i, s)
            start_step(i, s + 1)
    for c in range(chunks):
        stay[c].wait()

        @pl.loop(1, n_expert)
        def _(o):
            first(c, o).wait_recv()

        @pl.loop(0, n_expert)
        def _(o):
            source = match[(e + o) % n_expert]
            ordered[o, rows_of(c), :] = arrived[c][source]

        pltpu.make_async_copy(
            ordered.at[0, rows_of(c)], landed.at[e, rows_of(c)], own.at[1, c]
        ).start()

        @pl.loop(1, n_expert)
        def _(o):
            second(c, o).start()

    for s in range(early, steps):
        for i in range(halves):
            end_step(i, s)
            if s + 1 < steps:
                start_step(i, s + 1)
    for i in range(halves):
        result[pl.ds(i * half, half), :] = sums[i][steps - 1][...]
    for c in range(chunks):
        pltpu.make_async_copy(
            ordered.at[0, rows_of(c)], landed.at[e, rows_of(c)], own.at[1, c]
        ).wait()

        @pl.loop(1, n_expert)
        def _(o):
            second(c, o).wait_recv()
            first(c, o).wait_send()
            second(c, o).wait_send()

    for f in flights:
        for c in f:
            c.wait_send()


def exchange(n_expert, n_dp, matching, packed, part, tok_rows, width):
    expert_bits, dp_bits = bit_count(n_expert), bit_count(n_dp)
    steps = expert_bits + dp_bits
    chunks = 2 if packed.shape[1] % 32 == 0 else 1
    buffers = []
    for order in reduce_orders(expert_bits, dp_bits):
        for shape in reduce_shapes(order, expert_bits, dp_bits, tok_rows // 2, width):
            buffers.append(pltpu.VMEM(shape, part.dtype))
    return pl.pallas_call(
        functools.partial(exchange_kernel, n_expert, n_dp, chunks),
        out_shape=(
            jax.ShapeDtypeStruct(packed.shape, packed.dtype),
            jax.ShapeDtypeStruct((tok_rows, width), part.dtype),
        ),
        in_specs=[
            pl.BlockSpec(memory_space=pltpu.SMEM),
            pl.BlockSpec(memory_space=pltpu.VMEM),
            pl.BlockSpec(memory_space=pltpu.VMEM),
        ],
        out_specs=[pl.BlockSpec(memory_space=pltpu.VMEM)] * 2,
        scratch_shapes=buffers
        + buffers
        + [pltpu.VMEM((n_expert, packed.shape[1] // chunks, packed.shape[2]), packed.dtype)] * chunks
        + [
            pltpu.VMEM(packed.shape, packed.dtype),
            pltpu.SemaphoreType.DMA((chunks, n_expert)),
            pltpu.SemaphoreType.DMA((chunks, n_expert)),
            pltpu.SemaphoreType.DMA((chunks, n_expert)),
            pltpu.SemaphoreType.DMA((chunks, n_expert)),
            pltpu.SemaphoreType.DMA((2, chunks)),
            pltpu.SemaphoreType.DMA((2, steps)),
            pltpu.SemaphoreType.DMA((2, steps)),
        ],
        compiler_params=pltpu.CompilerParams(collective_id=1, has_side_effects=True),
    )(matching, packed, part.reshape((2,) * expert_bits + (tok_rows, part.shape[1])))


def column(table, index):
    lanes = lax.broadcasted_iota(jnp.int32, table.shape, 1)
    return jnp.sum(jnp.where(lanes == index, table, 0.0), axis=1)


def scaled(cotangent, weight):
    return (cotangent.astype(jnp.float32) * weight[:, None]).astype(jnp.bfloat16)


def selector(weight, blocks, capacity, kinds, slots):
    chosen = (weight > 0.0).reshape(blocks, -1)
    tok_rows = chosen.shape[1]
    at = lax.broadcasted_iota(jnp.int32, (tok_rows, tok_rows), 0)
    to = lax.broadcasted_iota(jnp.int32, (tok_rows, tok_rows), 1)
    upto = jnp.where(at <= to, 1.0, 0.0).astype(jnp.bfloat16)
    rank = jnp.dot(chosen.astype(jnp.bfloat16), upto, preferred_element_type=jnp.float32)
    rank = jnp.where(chosen, rank.astype(jnp.int32) - 1, -1)
    wide = jnp.concatenate([rank] * kinds, axis=1)[:, None, :]
    shape = (blocks, slots, kinds * tok_rows)
    slot = lax.broadcasted_iota(jnp.int32, shape, 1)
    kind = lax.broadcasted_iota(jnp.int32, shape, 2) // tok_rows
    hit = (wide >= 0) & (wide + kind * capacity == slot)
    return jnp.where(hit, 1.0, 0.0).astype(jnp.bfloat16)


def local(n_expert, n_dp, tokens, cotangent, routes, probs, matching, w_gate, w_up, w_down):
    experts = matching.shape[0]
    tok_rows, top_count = routes.shape
    w_gate, w_up, w_down = w_gate[0], w_up[0], w_down[0]
    hidden_width = w_gate.shape[1]
    capacity = max(2, 5 * tok_rows * top_count // (4 * experts))
    slots = -(-3 * capacity // 16) * 16
    me = lax.axis_index("expert")
    lanes = -(-experts // 128) * 128
    names = jnp.arange(lanes, dtype=jnp.int32)
    table = jnp.sum(
        jnp.where(routes[:, :, None] == names[None, None, :], probs[:, :, None], 0.0), axis=1
    )
    rows, cot, table = gather_all(n_expert, n_dp, tokens, cotangent, table)
    weight = column(table, me)
    grads = scaled(cot, weight)
    gate = jnp.dot(rows, w_gate, preferred_element_type=jnp.float32)
    upper = jnp.dot(rows, w_up, preferred_element_type=jnp.float32)
    sig = jax.nn.sigmoid(gate)
    hidden = (gate * sig * upper).astype(jnp.bfloat16)
    hidden_back = jnp.dot(grads, w_down, preferred_element_type=jnp.float32)
    up_back = (hidden_back * gate * sig).astype(jnp.bfloat16)
    gate_back = (hidden_back * upper * sig * (1.0 + gate * (1.0 - sig))).astype(jnp.bfloat16)
    cubes = [v.reshape(experts, tok_rows, hidden_width) for v in (gate_back, up_back, hidden)]
    stacked = jnp.concatenate(cubes, axis=1)
    pick = selector(weight, experts, capacity, 3, slots)
    packed = jnp.einsum(
        "jrt,jth->jrh", pick, stacked, preferred_element_type=jnp.float32
    ).astype(jnp.bfloat16)
    part = lax.dot_general(gate_back, w_gate, contract_cols, preferred_element_type=jnp.float32)
    part = part + lax.dot_general(up_back, w_up, contract_cols, preferred_element_type=jnp.float32)
    part = part.astype(jnp.bfloat16)
    landed, input_grad = exchange(
        n_expert, n_dp, matching, packed, part, tok_rows, tokens.shape[1]
    )
    partner = jnp.sum(jnp.where(jnp.arange(experts) == me, matching, 0))
    p_weight = column(table, partner)
    p_pick = selector(p_weight, experts, capacity, 3, slots)
    dense = jnp.einsum(
        "jrt,jrh->jth", p_pick, landed, preferred_element_type=jnp.float32
    ).astype(jnp.bfloat16)
    p_grads = scaled(cot, p_weight)
    total = experts * tok_rows

    def take(kind):
        return dense[:, kind * tok_rows : (kind + 1) * tok_rows].reshape(total, hidden_width)

    g_gate = lax.dot_general(rows, take(0), contract_rows, preferred_element_type=jnp.float32)
    g_up = lax.dot_general(rows, take(1), contract_rows, preferred_element_type=jnp.float32)
    g_down = lax.dot_general(p_grads, take(2), contract_rows, preferred_element_type=jnp.float32)
    return (input_grad, g_gate[None], g_up[None], g_down[None])


def solution(mesh):
    weights = P("expert", None, "dp")
    return jax.shard_map(
        functools.partial(local, mesh.shape["expert"], mesh.shape["dp"]),
        mesh=mesh,
        in_specs=(
            P("expert", "dp"),
            P("expert", "dp"),
            P("expert", None),
            P("expert", None),
            P(),
            weights,
            weights,
            weights,
        ),
        out_specs=(P("expert", "dp"), weights, weights, weights),
        check_vma=False,
    )
```

```python
import functools

import jax
import jax.numpy as jnp
from jax import lax
from jax.experimental import pallas as pl
from jax.experimental.pallas import tpu as pltpu
from jax.sharding import PartitionSpec as P

contract_rows = (((0,), (0,)), ((), ()))
contract_cols = (((1,), (1,)), ((), ()))
MESH = pl.DeviceIdType.MESH


def bit_count(size):
    return size.bit_length() - 1


def flipped(index, bit):
    step = 2**bit
    return index + step * (1 - 2 * ((index // step) % 2))


def gather_orders(expert_bits, dp_bits):
    far = [("expert", b) for b in range(expert_bits - 1, 1, -1)]
    mid = [("expert", 1)]
    last = [("expert", 0)]
    across = [("dp", b) for b in range(dp_bits)]
    return (
        far + across + mid + last,
        far + mid + across + last,
        across + far + mid + last,
        mid + far + across + last,
        far + mid + last,
    )


def gather_kernel(
    n_expert, n_dp, tokens, cotangent, table, all_tokens, all_cotangent, all_table, send, recv, own
):
    e = lax.axis_index("expert")
    d = lax.axis_index("dp")
    expert_bits, dp_bits = bit_count(n_expert), bit_count(n_dp)
    width = tokens.shape[1]
    half = tokens.shape[0] // 2

    def peer(axis, bit):
        if axis == "expert":
            return (d, flipped(e, bit))
        return (flipped(d, bit), e)

    def held(ref, done, rows, data):
        where = []
        for b in range(expert_bits - 1, -1, -1):
            where.append(slice(None) if ("expert", b) in done else (e // 2**b) % 2)
        where.append(rows)
        if data:
            k = len([x for x in done if x[0] == "dp"])
            start = pl.multiple_of((d // 2**k) * (2**k * width), width)
            where.append(pl.ds(start, 2**k * width))
        else:
            where.append(slice(None))
        return ref.at[tuple(where)]

    barrier = pltpu.get_barrier_semaphore()
    links = [("expert", b) for b in range(expert_bits)] + [("dp", b) for b in range(dp_bits)]
    for link in links:
        pl.semaphore_signal(barrier, inc=1, device_id=peer(*link), device_id_type=MESH)

    orders = gather_orders(expert_bits, dp_bits)
    top, low, whole = pl.ds(0, half), pl.ds(half, half), pl.ds(0, 2 * half)
    parts = [
        (tokens, all_tokens, top, orders[0], True),
        (tokens, all_tokens, low, orders[2], True),
        (cotangent, all_cotangent, top, orders[1], True),
        (cotangent, all_cotangent, low, orders[3], True),
        (table, all_table, whole, orders[4], False),
    ]
    locals_ = []
    for i, (src, dst, rows, order, data) in enumerate(parts):
        c = pltpu.make_async_copy(src.at[rows], held(dst, [], rows, data), own.at[i])
        c.start()
        locals_.append(c)
    pl.semaphore_wait(barrier, len(links))
    flights = [[] for _ in parts]
    steps = max(len(p[3]) for p in parts)
    for s in range(steps):
        turn = (4, 1, 3, 0, 2) if s < 2 else (4, 0, 2, 1, 3)
        for i in turn:
            src, dst, rows, order, data = parts[i]
            if s >= len(order):
                continue
            if s == 0:
                locals_[i].wait()
            else:
                flights[i][s - 1].wait_recv()
            block = held(dst, order[:s], rows, data)
            c = pltpu.make_async_remote_copy(
                src_ref=block,
                dst_ref=block,
                send_sem=send.at[i, s],
                recv_sem=recv.at[i, s],
                device_id=peer(*order[s]),
                device_id_type=MESH,
            )
            c.start()
            flights[i].append(c)
    for f in flights:
        f[-1].wait_recv()
        for c in f:
            c.wait_send()


def gather_all(n_expert, n_dp, tokens, cotangent, table):
    lead = (2,) * bit_count(n_expert)
    rows, width = tokens.shape
    steps = bit_count(n_expert) + bit_count(n_dp)
    wide = jax.ShapeDtypeStruct(lead + (rows, width * n_dp), tokens.dtype)
    small = jax.ShapeDtypeStruct(lead + table.shape, table.dtype)
    outs = pl.pallas_call(
        functools.partial(gather_kernel, n_expert, n_dp),
        out_shape=(wide, wide, small),
        in_specs=[pl.BlockSpec(memory_space=pltpu.VMEM)] * 3,
        out_specs=[pl.BlockSpec(memory_space=pl.ANY)] * 3,
        scratch_shapes=[
            pltpu.SemaphoreType.DMA((5, steps)),
            pltpu.SemaphoreType.DMA((5, steps)),
            pltpu.SemaphoreType.DMA((5,)),
        ],
        compiler_params=pltpu.CompilerParams(collective_id=0, has_side_effects=True),
    )(tokens, cotangent, table)
    total = n_expert * rows
    return (
        outs[0].reshape(total, width * n_dp),
        outs[1].reshape(total, width * n_dp),
        outs[2].reshape(total, table.shape[1]),
    )


def reduce_orders(expert_bits, dp_bits):
    far = [("expert", b) for b in range(2, expert_bits)]
    mid = [("expert", 1)]
    near = [("expert", 0)]
    across = [("dp", b) for b in range(dp_bits - 1, -1, -1)]
    return (near + across + mid + far, near + mid + across + far)


def reduce_shapes(order, expert_bits, dp_bits, rows, width):
    left_e, left_d = expert_bits, dp_bits
    shapes = []
    for axis, _ in order:
        if axis == "expert":
            left_e -= 1
        else:
            left_d -= 1
        shapes.append((2,) * left_e + (rows, width * 2**left_d))
    return shapes


def exchange_kernel(
    n_expert, n_dp, chunks, match, packed, g_back, u_back, w_gate, w_up, landed, result, *scratch
):
    e = lax.axis_index("expert")
    d = lax.axis_index("dp")
    expert_bits, dp_bits = bit_count(n_expert), bit_count(n_dp)
    steps = expert_bits + dp_bits
    halves = 2
    sums = [scratch[i * steps : (i + 1) * steps] for i in range(halves)]
    came = [scratch[(halves + i) * steps : (halves + i + 1) * steps] for i in range(halves)]
    rest = scratch[2 * halves * steps :]
    arrived = rest[:chunks]
    part, ordered, send1, recv1, send2, recv2, own, rsend, rrecv = rest[chunks:]
    size = packed.shape[1] // chunks
    width = result.shape[1]
    half = result.shape[0] // halves

    def peer(axis, bit):
        if axis == "expert":
            return (d, flipped(e, bit))
        return (flipped(d, bit), e)

    barrier = pltpu.get_barrier_semaphore()

    @pl.loop(1, n_expert)
    def _(o):
        pl.semaphore_signal(barrier, inc=1, device_id=(d, (e + o) % n_expert), device_id_type=MESH)

    for b in range(dp_bits):
        pl.semaphore_signal(barrier, inc=1, device_id=(flipped(d, b), e), device_id_type=MESH)

    def rows_of(c):
        return pl.ds(c * size, size)

    stay = [
        pltpu.make_async_copy(packed.at[e, rows_of(c)], arrived[c].at[e], own.at[0, c])
        for c in range(chunks)
    ]
    for c in stay:
        c.start()
    pl.semaphore_wait(barrier, n_expert - 1 + dp_bits)

    def first(c, o):
        to = (e + o) % n_expert
        return pltpu.make_async_remote_copy(
            src_ref=packed.at[to, rows_of(c)],
            dst_ref=arrived[c].at[e],
            send_sem=send1.at[c, o],
            recv_sem=recv1.at[c, o],
            device_id=(d, to),
            device_id_type=MESH,
        )

    def second(c, o):
        return pltpu.make_async_remote_copy(
            src_ref=ordered.at[o, rows_of(c)],
            dst_ref=landed.at[e, rows_of(c)],
            send_sem=send2.at[c, o],
            recv_sem=recv2.at[c, o],
            device_id=(d, (e + o) % n_expert),
            device_id_type=MESH,
        )

    orders = reduce_orders(expert_bits, dp_bits)
    flights = [[], []]

    def split(i, s):
        axis, bit = orders[i][s]
        if s == 0:
            ref, rows = part, pl.ds(i * half, half)
        else:
            ref, rows = sums[i][s - 1], slice(None)
        left = [b for a, b in orders[i][s:] if a == "expert"]
        left = sorted(left, reverse=True)
        if axis == "expert":
            mine = (e // 2**bit) % 2
            at = left.index(bit)

            def where(v):
                return tuple([slice(None)] * at + [v] + [slice(None)] * (len(left) - at - 1)) + (
                    rows,
                    slice(None),
                )

            return ref, where(mine), where(1 - mine)
        mine = (d // 2**bit) % 2
        span = 2**bit * width
        head = (slice(None),) * len(left) + (rows,)
        keep = head + (pl.ds(pl.multiple_of(mine * span, 128), span),)
        give = head + (pl.ds(pl.multiple_of((1 - mine) * span, 128), span),)
        return ref, keep, give

    def start_step(i, s):
        ref, _, give = split(i, s)
        c = pltpu.make_async_remote_copy(
            src_ref=ref.at[give],
            dst_ref=came[i][s],
            send_sem=rsend.at[i, s],
            recv_sem=rrecv.at[i, s],
            device_id=peer(*orders[i][s]),
            device_id_type=MESH,
        )
        c.start()
        flights[i].append(c)

    def end_step(i, s):
        ref, keep, _ = split(i, s)
        flights[i][s].wait_recv()
        total = ref[keep].astype(jnp.float32) + came[i][s][...].astype(jnp.float32)
        sums[i][s][...] = total.astype(sums[i][s].dtype)

    for c in range(chunks):

        @pl.loop(1, n_expert)
        def _(o):
            first(c, o).start()

    model_width = w_gate.shape[0]
    tile = min(512, model_width)
    for t in range(0, model_width, tile):
        piece = lax.dot_general(
            g_back[...], w_gate[t : t + tile], contract_cols, preferred_element_type=jnp.float32
        )
        piece += lax.dot_general(
            u_back[...], w_up[t : t + tile], contract_cols, preferred_element_type=jnp.float32
        )
        shape = part.shape[:-1] + (tile,)
        part[..., t : t + tile] = piece.astype(part.dtype).reshape(shape)
    for i in range(halves):
        start_step(i, 0)

    early = min(2, steps - 1)
    for s in range(early):
        for i in range(halves):
            end_step(i, s)
            start_step(i, s + 1)
    for c in range(chunks):
        stay[c].wait()

        @pl.loop(1, n_expert)
        def _(o):
            first(c, o).wait_recv()

        @pl.loop(0, n_expert)
        def _(o):
            source = match[(e + o) % n_expert]
            ordered[o, rows_of(c), :] = arrived[c][source]

        pltpu.make_async_copy(
            ordered.at[0, rows_of(c)], landed.at[e, rows_of(c)], own.at[1, c]
        ).start()

        @pl.loop(1, n_expert)
        def _(o):
            second(c, o).start()

    for s in range(early, steps):
        for i in range(halves):
            end_step(i, s)
            if s + 1 < steps:
                start_step(i, s + 1)
    for i in range(halves):
        result[pl.ds(i * half, half), :] = sums[i][steps - 1][...]
    for c in range(chunks):
        pltpu.make_async_copy(
            ordered.at[0, rows_of(c)], landed.at[e, rows_of(c)], own.at[1, c]
        ).wait()

        @pl.loop(1, n_expert)
        def _(o):
            second(c, o).wait_recv()
            first(c, o).wait_send()
            second(c, o).wait_send()

    for f in flights:
        for c in f:
            c.wait_send()


def exchange(n_expert, n_dp, matching, packed, g_back, u_back, w_gate, w_up, tok_rows, width):
    expert_bits, dp_bits = bit_count(n_expert), bit_count(n_dp)
    steps = expert_bits + dp_bits
    chunks = 2 if packed.shape[1] % 32 == 0 else 1
    buffers = []
    for order in reduce_orders(expert_bits, dp_bits):
        for shape in reduce_shapes(order, expert_bits, dp_bits, tok_rows // 2, width):
            buffers.append(pltpu.VMEM(shape, packed.dtype))
    return pl.pallas_call(
        functools.partial(exchange_kernel, n_expert, n_dp, chunks),
        out_shape=(
            jax.ShapeDtypeStruct(packed.shape, packed.dtype),
            jax.ShapeDtypeStruct((tok_rows, width), packed.dtype),
        ),
        in_specs=[
            pl.BlockSpec(memory_space=pltpu.SMEM),
        ]
        + [pl.BlockSpec(memory_space=pltpu.VMEM)] * 5,
        out_specs=[pl.BlockSpec(memory_space=pltpu.VMEM)] * 2,
        scratch_shapes=buffers
        + buffers
        + [pltpu.VMEM((n_expert, packed.shape[1] // chunks, packed.shape[2]), packed.dtype)] * chunks
        + [
            pltpu.VMEM((2,) * expert_bits + (tok_rows, w_gate.shape[0]), packed.dtype),
            pltpu.VMEM(packed.shape, packed.dtype),
            pltpu.SemaphoreType.DMA((chunks, n_expert)),
            pltpu.SemaphoreType.DMA((chunks, n_expert)),
            pltpu.SemaphoreType.DMA((chunks, n_expert)),
            pltpu.SemaphoreType.DMA((chunks, n_expert)),
            pltpu.SemaphoreType.DMA((2, chunks)),
            pltpu.SemaphoreType.DMA((2, steps)),
            pltpu.SemaphoreType.DMA((2, steps)),
        ],
        compiler_params=pltpu.CompilerParams(collective_id=1, has_side_effects=True),
    )(matching, packed, g_back, u_back, w_gate, w_up)


def column(table, index):
    lanes = lax.broadcasted_iota(jnp.int32, table.shape, 1)
    return jnp.sum(jnp.where(lanes == index, table, 0.0), axis=1)


def scaled(cotangent, weight):
    return (cotangent.astype(jnp.float32) * weight[:, None]).astype(jnp.bfloat16)


def selector(weight, blocks, capacity, kinds, slots):
    chosen = (weight > 0.0).reshape(blocks, -1)
    tok_rows = chosen.shape[1]
    at = lax.broadcasted_iota(jnp.int32, (tok_rows, tok_rows), 0)
    to = lax.broadcasted_iota(jnp.int32, (tok_rows, tok_rows), 1)
    upto = jnp.where(at <= to, 1.0, 0.0).astype(jnp.bfloat16)
    rank = jnp.dot(chosen.astype(jnp.bfloat16), upto, preferred_element_type=jnp.float32)
    rank = jnp.where(chosen, rank.astype(jnp.int32) - 1, -1)
    wide = jnp.concatenate([rank] * kinds, axis=1)[:, None, :]
    shape = (blocks, slots, kinds * tok_rows)
    slot = lax.broadcasted_iota(jnp.int32, shape, 1)
    kind = lax.broadcasted_iota(jnp.int32, shape, 2) // tok_rows
    hit = (wide >= 0) & (wide + kind * capacity == slot)
    return jnp.where(hit, 1.0, 0.0).astype(jnp.bfloat16)


def local(n_expert, n_dp, tokens, cotangent, routes, probs, matching, w_gate, w_up, w_down):
    experts = matching.shape[0]
    tok_rows, top_count = routes.shape
    w_gate, w_up, w_down = w_gate[0], w_up[0], w_down[0]
    hidden_width = w_gate.shape[1]
    capacity = max(2, 5 * tok_rows * top_count // (4 * experts))
    slots = -(-3 * capacity // 16) * 16
    me = lax.axis_index("expert")
    lanes = -(-experts // 128) * 128
    names = jnp.arange(lanes, dtype=jnp.int32)
    table = jnp.sum(
        jnp.where(routes[:, :, None] == names[None, None, :], probs[:, :, None], 0.0), axis=1
    )
    rows, cot, table = gather_all(n_expert, n_dp, tokens, cotangent, table)
    weight = column(table, me)
    grads = scaled(cot, weight)
    gate = jnp.dot(rows, w_gate, preferred_element_type=jnp.float32)
    upper = jnp.dot(rows, w_up, preferred_element_type=jnp.float32)
    sig = jax.nn.sigmoid(gate)
    hidden = (gate * sig * upper).astype(jnp.bfloat16)
    hidden_back = jnp.dot(grads, w_down, preferred_element_type=jnp.float32)
    up_back = (hidden_back * gate * sig).astype(jnp.bfloat16)
    gate_back = (hidden_back * upper * sig * (1.0 + gate * (1.0 - sig))).astype(jnp.bfloat16)
    cubes = [v.reshape(experts, tok_rows, hidden_width) for v in (gate_back, up_back, hidden)]
    stacked = jnp.concatenate(cubes, axis=1)
    pick = selector(weight, experts, capacity, 3, slots)
    packed = jnp.einsum(
        "jrt,jth->jrh", pick, stacked, preferred_element_type=jnp.float32
    ).astype(jnp.bfloat16)
    landed, input_grad = exchange(
        n_expert, n_dp, matching, packed, gate_back, up_back, w_gate, w_up, tok_rows, tokens.shape[1]
    )
    partner = jnp.sum(jnp.where(jnp.arange(experts) == me, matching, 0))
    p_weight = column(table, partner)
    p_pick = selector(p_weight, experts, capacity, 3, slots)
    dense = jnp.einsum(
        "jrt,jrh->jth", p_pick, landed, preferred_element_type=jnp.float32
    ).astype(jnp.bfloat16)
    p_grads = scaled(cot, p_weight)
    total = experts * tok_rows

    def take(kind):
        return dense[:, kind * tok_rows : (kind + 1) * tok_rows].reshape(total, hidden_width)

    g_gate = lax.dot_general(rows, take(0), contract_rows, preferred_element_type=jnp.float32)
    g_up = lax.dot_general(rows, take(1), contract_rows, preferred_element_type=jnp.float32)
    g_down = lax.dot_general(p_grads, take(2), contract_rows, preferred_element_type=jnp.float32)
    return (input_grad, g_gate[None], g_up[None], g_down[None])


def solution(mesh):
    weights = P("expert", None, "dp")
    return jax.shard_map(
        functools.partial(local, mesh.shape["expert"], mesh.shape["dp"]),
        mesh=mesh,
        in_specs=(
            P("expert", "dp"),
            P("expert", "dp"),
            P("expert", None),
            P("expert", None),
            P(),
            weights,
            weights,
            weights,
        ),
        out_specs=(P("expert", "dp"), weights, weights, weights),
        check_vma=False,
    )
```

```python
import functools

import jax
import jax.numpy as jnp
from jax import lax
from jax.experimental import pallas as pl
from jax.experimental.pallas import tpu as pltpu
from jax.sharding import PartitionSpec as P

contract_rows = (((0,), (0,)), ((), ()))
contract_cols = (((1,), (1,)), ((), ()))
MESH = pl.DeviceIdType.MESH


def bit_count(size):
    return size.bit_length() - 1


def flipped(index, bit):
    step = 2**bit
    return index + step * (1 - 2 * ((index // step) % 2))


def gather_orders(expert_bits, dp_bits):
    far = [("expert", b) for b in range(expert_bits - 1, 1, -1)]
    mid = [("expert", 1)]
    last = [("expert", 0)]
    across = [("dp", b) for b in range(dp_bits)]
    return (
        far + across + mid + last,
        far + mid + across + last,
        across + far + mid + last,
        mid + far + across + last,
        far + mid + last,
    )


def gather_kernel(
    n_expert, n_dp, tokens, cotangent, table, all_tokens, all_cotangent, all_table, send, recv, own
):
    e = lax.axis_index("expert")
    d = lax.axis_index("dp")
    expert_bits, dp_bits = bit_count(n_expert), bit_count(n_dp)
    width = tokens.shape[1]
    half = tokens.shape[0] // 2

    def peer(axis, bit):
        if axis == "expert":
            return (d, flipped(e, bit))
        return (flipped(d, bit), e)

    def held(ref, done, rows, data):
        where = []
        for b in range(expert_bits - 1, -1, -1):
            where.append(slice(None) if ("expert", b) in done else (e // 2**b) % 2)
        where.append(rows)
        if data:
            k = len([x for x in done if x[0] == "dp"])
            start = pl.multiple_of((d // 2**k) * (2**k * width), width)
            where.append(pl.ds(start, 2**k * width))
        else:
            where.append(slice(None))
        return ref.at[tuple(where)]

    barrier = pltpu.get_barrier_semaphore()
    links = [("expert", b) for b in range(expert_bits)] + [("dp", b) for b in range(dp_bits)]
    for link in links:
        pl.semaphore_signal(barrier, inc=1, device_id=peer(*link), device_id_type=MESH)

    orders = gather_orders(expert_bits, dp_bits)
    top, low, whole = pl.ds(0, half), pl.ds(half, half), pl.ds(0, 2 * half)
    parts = [
        (tokens, all_tokens, top, orders[0], True),
        (tokens, all_tokens, low, orders[2], True),
        (cotangent, all_cotangent, top, orders[1], True),
        (cotangent, all_cotangent, low, orders[3], True),
        (table, all_table, whole, orders[4], False),
    ]
    locals_ = []
    for i, (src, dst, rows, order, data) in enumerate(parts):
        c = pltpu.make_async_copy(src.at[rows], held(dst, [], rows, data), own.at[i])
        c.start()
        locals_.append(c)
    pl.semaphore_wait(barrier, len(links))
    flights = [[] for _ in parts]
    steps = max(len(p[3]) for p in parts)
    for s in range(steps):
        turn = (4, 1, 3, 0, 2) if s < 2 else (4, 0, 2, 1, 3)
        for i in turn:
            src, dst, rows, order, data = parts[i]
            if s >= len(order):
                continue
            if s == 0:
                locals_[i].wait()
            else:
                flights[i][s - 1].wait_recv()
            block = held(dst, order[:s], rows, data)
            c = pltpu.make_async_remote_copy(
                src_ref=block,
                dst_ref=block,
                send_sem=send.at[i, s],
                recv_sem=recv.at[i, s],
                device_id=peer(*order[s]),
                device_id_type=MESH,
            )
            c.start()
            flights[i].append(c)
    for f in flights:
        f[-1].wait_recv()
        for c in f:
            c.wait_send()


def gather_all(n_expert, n_dp, tokens, cotangent, table):
    lead = (2,) * bit_count(n_expert)
    rows, width = tokens.shape
    steps = bit_count(n_expert) + bit_count(n_dp)
    wide = jax.ShapeDtypeStruct(lead + (rows, width * n_dp), tokens.dtype)
    small = jax.ShapeDtypeStruct(lead + table.shape, table.dtype)
    outs = pl.pallas_call(
        functools.partial(gather_kernel, n_expert, n_dp),
        out_shape=(wide, wide, small),
        in_specs=[pl.BlockSpec(memory_space=pltpu.VMEM)] * 3,
        out_specs=[pl.BlockSpec(memory_space=pltpu.VMEM)] * 3,
        scratch_shapes=[
            pltpu.SemaphoreType.DMA((5, steps)),
            pltpu.SemaphoreType.DMA((5, steps)),
            pltpu.SemaphoreType.DMA((5,)),
        ],
        compiler_params=pltpu.CompilerParams(collective_id=0, has_side_effects=True),
    )(tokens, cotangent, table)
    total = n_expert * rows
    return (
        outs[0].reshape(total, width * n_dp),
        outs[1].reshape(total, width * n_dp),
        outs[2].reshape(total, table.shape[1]),
    )


def reduce_orders(expert_bits, dp_bits):
    far = [("expert", b) for b in range(2, expert_bits)]
    mid = [("expert", 1)]
    near = [("expert", 0)]
    across = [("dp", b) for b in range(dp_bits - 1, -1, -1)]
    return (near + across + mid + far, near + mid + across + far)


def reduce_shapes(order, expert_bits, dp_bits, rows, width):
    left_e, left_d = expert_bits, dp_bits
    shapes = []
    for axis, _ in order:
        if axis == "expert":
            left_e -= 1
        else:
            left_d -= 1
        shapes.append((2,) * left_e + (rows, width * 2**left_d))
    return shapes


def exchange_kernel(
    n_expert, n_dp, chunks, match, packed, g_back, u_back, w_gate, w_up, landed, result, *scratch
):
    e = lax.axis_index("expert")
    d = lax.axis_index("dp")
    expert_bits, dp_bits = bit_count(n_expert), bit_count(n_dp)
    steps = expert_bits + dp_bits
    halves = 2
    sums = [scratch[i * steps : (i + 1) * steps] for i in range(halves)]
    came = [scratch[(halves + i) * steps : (halves + i + 1) * steps] for i in range(halves)]
    rest = scratch[2 * halves * steps :]
    arrived = rest[:chunks]
    part, ordered, send1, recv1, send2, recv2, own, rsend, rrecv = rest[chunks:]
    size = packed.shape[1] // chunks
    width = result.shape[1]
    half = result.shape[0] // halves

    def peer(axis, bit):
        if axis == "expert":
            return (d, flipped(e, bit))
        return (flipped(d, bit), e)

    barrier = pltpu.get_barrier_semaphore()

    @pl.loop(1, n_expert)
    def _(o):
        pl.semaphore_signal(barrier, inc=1, device_id=(d, (e + o) % n_expert), device_id_type=MESH)

    for b in range(dp_bits):
        pl.semaphore_signal(barrier, inc=1, device_id=(flipped(d, b), e), device_id_type=MESH)

    def rows_of(c):
        return pl.ds(c * size, size)

    stay = [
        pltpu.make_async_copy(packed.at[e, rows_of(c)], arrived[c].at[e], own.at[0, c])
        for c in range(chunks)
    ]
    for c in stay:
        c.start()
    pl.semaphore_wait(barrier, n_expert - 1 + dp_bits)

    def first(c, o):
        to = (e + o) % n_expert
        return pltpu.make_async_remote_copy(
            src_ref=packed.at[to, rows_of(c)],
            dst_ref=arrived[c].at[e],
            send_sem=send1.at[c, o],
            recv_sem=recv1.at[c, o],
            device_id=(d, to),
            device_id_type=MESH,
        )

    def second(c, o):
        return pltpu.make_async_remote_copy(
            src_ref=ordered.at[o, rows_of(c)],
            dst_ref=landed.at[e, rows_of(c)],
            send_sem=send2.at[c, o],
            recv_sem=recv2.at[c, o],
            device_id=(d, (e + o) % n_expert),
            device_id_type=MESH,
        )

    orders = reduce_orders(expert_bits, dp_bits)
    flights = [[], []]

    def split(i, s):
        axis, bit = orders[i][s]
        if s == 0:
            ref, rows = part, pl.ds(i * half, half)
        else:
            ref, rows = sums[i][s - 1], slice(None)
        left = [b for a, b in orders[i][s:] if a == "expert"]
        left = sorted(left, reverse=True)
        if axis == "expert":
            mine = (e // 2**bit) % 2
            at = left.index(bit)

            def where(v):
                return tuple([slice(None)] * at + [v] + [slice(None)] * (len(left) - at - 1)) + (
                    rows,
                    slice(None),
                )

            return ref, where(mine), where(1 - mine)
        mine = (d // 2**bit) % 2
        span = 2**bit * width
        head = (slice(None),) * len(left) + (rows,)
        keep = head + (pl.ds(pl.multiple_of(mine * span, 128), span),)
        give = head + (pl.ds(pl.multiple_of((1 - mine) * span, 128), span),)
        return ref, keep, give

    def start_step(i, s):
        ref, _, give = split(i, s)
        c = pltpu.make_async_remote_copy(
            src_ref=ref.at[give],
            dst_ref=came[i][s],
            send_sem=rsend.at[i, s],
            recv_sem=rrecv.at[i, s],
            device_id=peer(*orders[i][s]),
            device_id_type=MESH,
        )
        c.start()
        flights[i].append(c)

    def end_step(i, s):
        ref, keep, _ = split(i, s)
        flights[i][s].wait_recv()
        total = ref[keep].astype(jnp.float32) + came[i][s][...].astype(jnp.float32)
        sums[i][s][...] = total.astype(sums[i][s].dtype)

    for c in range(chunks):

        @pl.loop(1, n_expert)
        def _(o):
            first(c, o).start()

    model_width = w_gate.shape[0]
    tile = min(512, model_width)
    for t in range(0, model_width, tile):
        piece = lax.dot_general(
            g_back[...], w_gate[t : t + tile], contract_cols, preferred_element_type=jnp.float32
        )
        piece += lax.dot_general(
            u_back[...], w_up[t : t + tile], contract_cols, preferred_element_type=jnp.float32
        )
        shape = part.shape[:-1] + (tile,)
        part[..., t : t + tile] = piece.astype(part.dtype).reshape(shape)
    for i in range(halves):
        start_step(i, 0)

    early = min(2, steps - 1)
    for s in range(early):
        for i in range(halves):
            end_step(i, s)
            start_step(i, s + 1)
    for c in range(chunks):
        stay[c].wait()

        @pl.loop(1, n_expert)
        def _(o):
            first(c, o).wait_recv()

        @pl.loop(0, n_expert)
        def _(o):
            source = match[(e + o) % n_expert]
            ordered[o, rows_of(c), :] = arrived[c][source]

        pltpu.make_async_copy(
            ordered.at[0, rows_of(c)], landed.at[e, rows_of(c)], own.at[1, c]
        ).start()

        @pl.loop(1, n_expert)
        def _(o):
            second(c, o).start()

    for s in range(early, steps):
        for i in range(halves):
            end_step(i, s)
            if s + 1 < steps:
                start_step(i, s + 1)
    for i in range(halves):
        result[pl.ds(i * half, half), :] = sums[i][steps - 1][...]
    for c in range(chunks):
        pltpu.make_async_copy(
            ordered.at[0, rows_of(c)], landed.at[e, rows_of(c)], own.at[1, c]
        ).wait()

        @pl.loop(1, n_expert)
        def _(o):
            second(c, o).wait_recv()
            first(c, o).wait_send()
            second(c, o).wait_send()

    for f in flights:
        for c in f:
            c.wait_send()


def exchange(n_expert, n_dp, matching, packed, g_back, u_back, w_gate, w_up, tok_rows, width):
    expert_bits, dp_bits = bit_count(n_expert), bit_count(n_dp)
    steps = expert_bits + dp_bits
    chunks = 2 if packed.shape[1] % 32 == 0 else 1
    buffers = []
    for order in reduce_orders(expert_bits, dp_bits):
        for shape in reduce_shapes(order, expert_bits, dp_bits, tok_rows // 2, width):
            buffers.append(pltpu.VMEM(shape, packed.dtype))
    return pl.pallas_call(
        functools.partial(exchange_kernel, n_expert, n_dp, chunks),
        out_shape=(
            jax.ShapeDtypeStruct(packed.shape, packed.dtype),
            jax.ShapeDtypeStruct((tok_rows, width), packed.dtype),
        ),
        in_specs=[
            pl.BlockSpec(memory_space=pltpu.SMEM),
        ]
        + [pl.BlockSpec(memory_space=pltpu.VMEM)] * 5,
        out_specs=[pl.BlockSpec(memory_space=pltpu.VMEM)] * 2,
        scratch_shapes=buffers
        + buffers
        + [pltpu.VMEM((n_expert, packed.shape[1] // chunks, packed.shape[2]), packed.dtype)] * chunks
        + [
            pltpu.VMEM((2,) * expert_bits + (tok_rows, w_gate.shape[0]), packed.dtype),
            pltpu.VMEM(packed.shape, packed.dtype),
            pltpu.SemaphoreType.DMA((chunks, n_expert)),
            pltpu.SemaphoreType.DMA((chunks, n_expert)),
            pltpu.SemaphoreType.DMA((chunks, n_expert)),
            pltpu.SemaphoreType.DMA((chunks, n_expert)),
            pltpu.SemaphoreType.DMA((2, chunks)),
            pltpu.SemaphoreType.DMA((2, steps)),
            pltpu.SemaphoreType.DMA((2, steps)),
        ],
        compiler_params=pltpu.CompilerParams(collective_id=1, has_side_effects=True),
    )(matching, packed, g_back, u_back, w_gate, w_up)


def column(table, index):
    lanes = lax.broadcasted_iota(jnp.int32, table.shape, 1)
    return jnp.sum(jnp.where(lanes == index, table, 0.0), axis=1)


def scaled(cotangent, weight):
    return (cotangent.astype(jnp.float32) * weight[:, None]).astype(jnp.bfloat16)


def selector(weight, blocks, capacity, kinds, slots):
    chosen = (weight > 0.0).reshape(blocks, -1)
    tok_rows = chosen.shape[1]
    at = lax.broadcasted_iota(jnp.int32, (tok_rows, tok_rows), 0)
    to = lax.broadcasted_iota(jnp.int32, (tok_rows, tok_rows), 1)
    upto = jnp.where(at <= to, 1.0, 0.0).astype(jnp.bfloat16)
    rank = jnp.dot(chosen.astype(jnp.bfloat16), upto, preferred_element_type=jnp.float32)
    rank = jnp.where(chosen, rank.astype(jnp.int32) - 1, -1)
    wide = jnp.concatenate([rank] * kinds, axis=1)[:, None, :]
    shape = (blocks, slots, kinds * tok_rows)
    slot = lax.broadcasted_iota(jnp.int32, shape, 1)
    kind = lax.broadcasted_iota(jnp.int32, shape, 2) // tok_rows
    hit = (wide >= 0) & (wide + kind * capacity == slot)
    return jnp.where(hit, 1.0, 0.0).astype(jnp.bfloat16)


def local(n_expert, n_dp, tokens, cotangent, routes, probs, matching, w_gate, w_up, w_down):
    experts = matching.shape[0]
    tok_rows, top_count = routes.shape
    w_gate, w_up, w_down = w_gate[0], w_up[0], w_down[0]
    hidden_width = w_gate.shape[1]
    capacity = max(2, 5 * tok_rows * top_count // (4 * experts))
    slots = -(-3 * capacity // 16) * 16
    me = lax.axis_index("expert")
    lanes = -(-experts // 128) * 128
    names = jnp.arange(lanes, dtype=jnp.int32)
    table = jnp.sum(
        jnp.where(routes[:, :, None] == names[None, None, :], probs[:, :, None], 0.0), axis=1
    )
    rows, cot, table = gather_all(n_expert, n_dp, tokens, cotangent, table)
    weight = column(table, me)
    grads = scaled(cot, weight)
    gate = jnp.dot(rows, w_gate, preferred_element_type=jnp.float32)
    upper = jnp.dot(rows, w_up, preferred_element_type=jnp.float32)
    sig = jax.nn.sigmoid(gate)
    hidden = (gate * sig * upper).astype(jnp.bfloat16)
    hidden_back = jnp.dot(grads, w_down, preferred_element_type=jnp.float32)
    up_back = (hidden_back * gate * sig).astype(jnp.bfloat16)
    gate_back = (hidden_back * upper * sig * (1.0 + gate * (1.0 - sig))).astype(jnp.bfloat16)
    cubes = [v.reshape(experts, tok_rows, hidden_width) for v in (gate_back, up_back, hidden)]
    stacked = jnp.concatenate(cubes, axis=1)
    pick = selector(weight, experts, capacity, 3, slots)
    packed = jnp.einsum(
        "jrt,jth->jrh", pick, stacked, preferred_element_type=jnp.float32
    ).astype(jnp.bfloat16)
    landed, input_grad = exchange(
        n_expert, n_dp, matching, packed, gate_back, up_back, w_gate, w_up, tok_rows, tokens.shape[1]
    )
    partner = jnp.sum(jnp.where(jnp.arange(experts) == me, matching, 0))
    p_weight = column(table, partner)
    p_pick = selector(p_weight, experts, capacity, 3, slots)
    dense = jnp.einsum(
        "jrt,jrh->jth", p_pick, landed, preferred_element_type=jnp.float32
    ).astype(jnp.bfloat16)
    p_grads = scaled(cot, p_weight)
    total = experts * tok_rows

    def take(kind):
        return dense[:, kind * tok_rows : (kind + 1) * tok_rows].reshape(total, hidden_width)

    g_gate = lax.dot_general(rows, take(0), contract_rows, preferred_element_type=jnp.float32)
    g_up = lax.dot_general(rows, take(1), contract_rows, preferred_element_type=jnp.float32)
    g_down = lax.dot_general(p_grads, take(2), contract_rows, preferred_element_type=jnp.float32)
    return (input_grad, g_gate[None], g_up[None], g_down[None])


def solution(mesh):
    weights = P("expert", None, "dp")
    return jax.shard_map(
        functools.partial(local, mesh.shape["expert"], mesh.shape["dp"]),
        mesh=mesh,
        in_specs=(
            P("expert", "dp"),
            P("expert", "dp"),
            P("expert", None),
            P("expert", None),
            P(),
            weights,
            weights,
            weights,
        ),
        out_specs=(P("expert", "dp"), weights, weights, weights),
        check_vma=False,
    )
```

```python
import functools

import jax
import jax.numpy as jnp
from jax import lax
from jax.experimental import pallas as pl
from jax.experimental.pallas import tpu as pltpu
from jax.sharding import PartitionSpec as P

contract_rows = (((0,), (0,)), ((), ()))
contract_cols = (((1,), (1,)), ((), ()))
MESH = pl.DeviceIdType.MESH


def bit_count(size):
    return size.bit_length() - 1


def flipped(index, bit):
    step = 2**bit
    return index + step * (1 - 2 * ((index // step) % 2))


def gather_orders(expert_bits, dp_bits):
    far = [("expert", b) for b in range(expert_bits - 1, 1, -1)]
    mid = [("expert", 1)]
    last = [("expert", 0)]
    across = [("dp", b) for b in range(dp_bits)]
    return (
        far + across + mid + last,
        far + mid + across + last,
        across + far + mid + last,
        mid + far + across + last,
        far + mid + last,
    )


def gather_kernel(
    n_expert, n_dp, tokens, cotangent, table, all_tokens, all_cotangent, all_table, send, recv, own
):
    e = lax.axis_index("expert")
    d = lax.axis_index("dp")
    expert_bits, dp_bits = bit_count(n_expert), bit_count(n_dp)
    width = tokens.shape[1]
    half = tokens.shape[0] // 2

    def peer(axis, bit):
        if axis == "expert":
            return (d, flipped(e, bit))
        return (flipped(d, bit), e)

    def held(ref, done, rows, data):
        where = []
        for b in range(expert_bits - 1, -1, -1):
            where.append(slice(None) if ("expert", b) in done else (e // 2**b) % 2)
        where.append(rows)
        if data:
            k = len([x for x in done if x[0] == "dp"])
            start = pl.multiple_of((d // 2**k) * (2**k * width), width)
            where.append(pl.ds(start, 2**k * width))
        else:
            where.append(slice(None))
        return ref.at[tuple(where)]

    barrier = pltpu.get_barrier_semaphore()
    links = [("expert", b) for b in range(expert_bits)] + [("dp", b) for b in range(dp_bits)]
    for link in links:
        pl.semaphore_signal(barrier, inc=1, device_id=peer(*link), device_id_type=MESH)

    orders = gather_orders(expert_bits, dp_bits)
    top, low, whole = pl.ds(0, half), pl.ds(half, half), pl.ds(0, 2 * half)
    parts = [
        (tokens, all_tokens, top, orders[0], True),
        (tokens, all_tokens, low, orders[2], True),
        (cotangent, all_cotangent, top, orders[1], True),
        (cotangent, all_cotangent, low, orders[3], True),
        (table, all_table, whole, orders[4], False),
    ]
    locals_ = []
    for i, (src, dst, rows, order, data) in enumerate(parts):
        c = pltpu.make_async_copy(src.at[rows], held(dst, [], rows, data), own.at[i])
        c.start()
        locals_.append(c)
    pl.semaphore_wait(barrier, len(links))
    flights = [[] for _ in parts]
    steps = max(len(p[3]) for p in parts)
    for s in range(steps):
        turn = (4, 1, 3, 0, 2) if s < 2 else (4, 0, 2, 1, 3)
        for i in turn:
            src, dst, rows, order, data = parts[i]
            if s >= len(order):
                continue
            if s == 0:
                locals_[i].wait()
            else:
                flights[i][s - 1].wait_recv()
            block = held(dst, order[:s], rows, data)
            c = pltpu.make_async_remote_copy(
                src_ref=block,
                dst_ref=block,
                send_sem=send.at[i, s],
                recv_sem=recv.at[i, s],
                device_id=peer(*order[s]),
                device_id_type=MESH,
            )
            c.start()
            flights[i].append(c)
    for f in flights:
        f[-1].wait_recv()
        for c in f:
            c.wait_send()


def gather_all(n_expert, n_dp, tokens, cotangent, table):
    lead = (2,) * bit_count(n_expert)
    rows, width = tokens.shape
    steps = bit_count(n_expert) + bit_count(n_dp)
    wide = jax.ShapeDtypeStruct(lead + (rows, width * n_dp), tokens.dtype)
    small = jax.ShapeDtypeStruct(lead + table.shape, table.dtype)
    outs = pl.pallas_call(
        functools.partial(gather_kernel, n_expert, n_dp),
        out_shape=(wide, wide, small),
        in_specs=[pl.BlockSpec(memory_space=pltpu.VMEM)] * 3,
        out_specs=[pl.BlockSpec(memory_space=pltpu.VMEM)] * 3,
        scratch_shapes=[
            pltpu.SemaphoreType.DMA((5, steps)),
            pltpu.SemaphoreType.DMA((5, steps)),
            pltpu.SemaphoreType.DMA((5,)),
        ],
        compiler_params=pltpu.CompilerParams(collective_id=0, has_side_effects=True),
    )(tokens, cotangent, table)
    total = n_expert * rows
    return (
        outs[0].reshape(total, width * n_dp),
        outs[1].reshape(total, width * n_dp),
        outs[2].reshape(total, table.shape[1]),
    )


def reduce_orders(expert_bits, dp_bits):
    far = [("expert", b) for b in range(2, expert_bits)]
    mid = [("expert", 1)]
    near = [("expert", 0)]
    across = [("dp", b) for b in range(dp_bits - 1, -1, -1)]
    return (near + across + mid + far, near + mid + across + far)


def reduce_shapes(order, expert_bits, dp_bits, rows, width):
    left_e, left_d = expert_bits, dp_bits
    shapes = []
    for axis, _ in order:
        if axis == "expert":
            left_e -= 1
        else:
            left_d -= 1
        shapes.append((2,) * left_e + (rows, width * 2**left_d))
    return shapes


def exchange_kernel(
    n_expert, n_dp, chunks, match, packed, g_back, u_back, w_gate, w_up, landed, result, *scratch
):
    e = lax.axis_index("expert")
    d = lax.axis_index("dp")
    expert_bits, dp_bits = bit_count(n_expert), bit_count(n_dp)
    steps = expert_bits + dp_bits
    halves = 2
    sums = [scratch[i * steps : (i + 1) * steps] for i in range(halves)]
    came = [scratch[(halves + i) * steps : (halves + i + 1) * steps] for i in range(halves)]
    rest = scratch[2 * halves * steps :]
    arrived = rest[:chunks]
    part, ordered, send1, recv1, send2, recv2, own, rsend, rrecv = rest[chunks:]
    size = packed.shape[1] // chunks
    width = result.shape[1]
    half = result.shape[0] // halves

    def peer(axis, bit):
        if axis == "expert":
            return (d, flipped(e, bit))
        return (flipped(d, bit), e)

    barrier = pltpu.get_barrier_semaphore()

    @pl.loop(1, n_expert)
    def _(o):
        pl.semaphore_signal(barrier, inc=1, device_id=(d, (e + o) % n_expert), device_id_type=MESH)

    for b in range(dp_bits):
        pl.semaphore_signal(barrier, inc=1, device_id=(flipped(d, b), e), device_id_type=MESH)

    def rows_of(c):
        return pl.ds(c * size, size)

    stay = [
        pltpu.make_async_copy(packed.at[e, rows_of(c)], arrived[c].at[e], own.at[0, c])
        for c in range(chunks)
    ]
    for c in stay:
        c.start()
    pl.semaphore_wait(barrier, n_expert - 1 + dp_bits)

    def first(c, o):
        to = (e + o) % n_expert
        return pltpu.make_async_remote_copy(
            src_ref=packed.at[to, rows_of(c)],
            dst_ref=arrived[c].at[e],
            send_sem=send1.at[c, o],
            recv_sem=recv1.at[c, o],
            device_id=(d, to),
            device_id_type=MESH,
        )

    def second(c, o):
        return pltpu.make_async_remote_copy(
            src_ref=ordered.at[o, rows_of(c)],
            dst_ref=landed.at[e, rows_of(c)],
            send_sem=send2.at[c, o],
            recv_sem=recv2.at[c, o],
            device_id=(d, (e + o) % n_expert),
            device_id_type=MESH,
        )

    orders = reduce_orders(expert_bits, dp_bits)
    flights = [[], []]

    def split(i, s):
        axis, bit = orders[i][s]
        if s == 0:
            ref, rows = part, pl.ds(i * half, half)
        else:
            ref, rows = sums[i][s - 1], slice(None)
        left = [b for a, b in orders[i][s:] if a == "expert"]
        left = sorted(left, reverse=True)
        if axis == "expert":
            mine = (e // 2**bit) % 2
            at = left.index(bit)

            def where(v):
                return tuple([slice(None)] * at + [v] + [slice(None)] * (len(left) - at - 1)) + (
                    rows,
                    slice(None),
                )

            return ref, where(mine), where(1 - mine)
        mine = (d // 2**bit) % 2
        span = 2**bit * width
        head = (slice(None),) * len(left) + (rows,)
        keep = head + (pl.ds(pl.multiple_of(mine * span, 128), span),)
        give = head + (pl.ds(pl.multiple_of((1 - mine) * span, 128), span),)
        return ref, keep, give

    def start_step(i, s):
        ref, _, give = split(i, s)
        c = pltpu.make_async_remote_copy(
            src_ref=ref.at[give],
            dst_ref=came[i][s],
            send_sem=rsend.at[i, s],
            recv_sem=rrecv.at[i, s],
            device_id=peer(*orders[i][s]),
            device_id_type=MESH,
        )
        c.start()
        flights[i].append(c)

    def end_step(i, s):
        ref, keep, _ = split(i, s)
        flights[i][s].wait_recv()
        total = ref[keep].astype(jnp.float32) + came[i][s][...].astype(jnp.float32)
        sums[i][s][...] = total.astype(sums[i][s].dtype)

    for c in range(chunks):

        @pl.loop(1, n_expert)
        def _(o):
            first(c, o).start()

    model_width = w_gate.shape[0]
    tile = min(512, model_width)
    for t in range(0, model_width, tile):
        piece = lax.dot_general(
            g_back[...], w_gate[t : t + tile], contract_cols, preferred_element_type=jnp.float32
        )
        piece += lax.dot_general(
            u_back[...], w_up[t : t + tile], contract_cols, preferred_element_type=jnp.float32
        )
        shape = part.shape[:-1] + (tile,)
        part[..., t : t + tile] = piece.astype(part.dtype).reshape(shape)
    for i in range(halves):
        start_step(i, 0)

    early = steps - 2
    for s in range(early):
        for i in range(halves):
            end_step(i, s)
            start_step(i, s + 1)
    for c in range(chunks):
        stay[c].wait()

        @pl.loop(1, n_expert)
        def _(o):
            first(c, o).wait_recv()

        @pl.loop(0, n_expert)
        def _(o):
            source = match[(e + o) % n_expert]
            ordered[o, rows_of(c), :] = arrived[c][source]

        pltpu.make_async_copy(
            ordered.at[0, rows_of(c)], landed.at[e, rows_of(c)], own.at[1, c]
        ).start()
        if c == chunks - 1:
            for i in range(halves):
                end_step(i, early)
                start_step(i, early + 1)

        @pl.loop(1, n_expert)
        def _(o):
            second(c, o).start()

    for i in range(halves):
        end_step(i, steps - 1)
    for i in range(halves):
        result[pl.ds(i * half, half), :] = sums[i][steps - 1][...]
    for c in range(chunks):
        pltpu.make_async_copy(
            ordered.at[0, rows_of(c)], landed.at[e, rows_of(c)], own.at[1, c]
        ).wait()

        @pl.loop(1, n_expert)
        def _(o):
            second(c, o).wait_recv()
            first(c, o).wait_send()
            second(c, o).wait_send()

    for f in flights:
        for c in f:
            c.wait_send()


def exchange(n_expert, n_dp, matching, packed, g_back, u_back, w_gate, w_up, tok_rows, width):
    expert_bits, dp_bits = bit_count(n_expert), bit_count(n_dp)
    steps = expert_bits + dp_bits
    chunks = 2 if packed.shape[1] % 32 == 0 else 1
    buffers = []
    for order in reduce_orders(expert_bits, dp_bits):
        for shape in reduce_shapes(order, expert_bits, dp_bits, tok_rows // 2, width):
            buffers.append(pltpu.VMEM(shape, packed.dtype))
    return pl.pallas_call(
        functools.partial(exchange_kernel, n_expert, n_dp, chunks),
        out_shape=(
            jax.ShapeDtypeStruct(packed.shape, packed.dtype),
            jax.ShapeDtypeStruct((tok_rows, width), packed.dtype),
        ),
        in_specs=[
            pl.BlockSpec(memory_space=pltpu.SMEM),
        ]
        + [pl.BlockSpec(memory_space=pltpu.VMEM)] * 5,
        out_specs=[pl.BlockSpec(memory_space=pltpu.VMEM)] * 2,
        scratch_shapes=buffers
        + buffers
        + [pltpu.VMEM((n_expert, packed.shape[1] // chunks, packed.shape[2]), packed.dtype)] * chunks
        + [
            pltpu.VMEM((2,) * expert_bits + (tok_rows, w_gate.shape[0]), packed.dtype),
            pltpu.VMEM(packed.shape, packed.dtype),
            pltpu.SemaphoreType.DMA((chunks, n_expert)),
            pltpu.SemaphoreType.DMA((chunks, n_expert)),
            pltpu.SemaphoreType.DMA((chunks, n_expert)),
            pltpu.SemaphoreType.DMA((chunks, n_expert)),
            pltpu.SemaphoreType.DMA((2, chunks)),
            pltpu.SemaphoreType.DMA((2, steps)),
            pltpu.SemaphoreType.DMA((2, steps)),
        ],
        compiler_params=pltpu.CompilerParams(collective_id=1, has_side_effects=True),
    )(matching, packed, g_back, u_back, w_gate, w_up)


def column(table, index):
    lanes = lax.broadcasted_iota(jnp.int32, table.shape, 1)
    return jnp.sum(jnp.where(lanes == index, table, 0.0), axis=1)


def scaled(cotangent, weight):
    return (cotangent.astype(jnp.float32) * weight[:, None]).astype(jnp.bfloat16)


def selector(weight, blocks, capacity, kinds, slots):
    chosen = (weight > 0.0).reshape(blocks, -1)
    tok_rows = chosen.shape[1]
    at = lax.broadcasted_iota(jnp.int32, (tok_rows, tok_rows), 0)
    to = lax.broadcasted_iota(jnp.int32, (tok_rows, tok_rows), 1)
    upto = jnp.where(at <= to, 1.0, 0.0).astype(jnp.bfloat16)
    rank = jnp.dot(chosen.astype(jnp.bfloat16), upto, preferred_element_type=jnp.float32)
    rank = jnp.where(chosen, rank.astype(jnp.int32) - 1, -1)
    wide = jnp.concatenate([rank] * kinds, axis=1)[:, None, :]
    shape = (blocks, slots, kinds * tok_rows)
    slot = lax.broadcasted_iota(jnp.int32, shape, 1)
    kind = lax.broadcasted_iota(jnp.int32, shape, 2) // tok_rows
    hit = (wide >= 0) & (wide + kind * capacity == slot)
    return jnp.where(hit, 1.0, 0.0).astype(jnp.bfloat16)


def local(n_expert, n_dp, tokens, cotangent, routes, probs, matching, w_gate, w_up, w_down):
    experts = matching.shape[0]
    tok_rows, top_count = routes.shape
    w_gate, w_up, w_down = w_gate[0], w_up[0], w_down[0]
    hidden_width = w_gate.shape[1]
    capacity = max(2, 5 * tok_rows * top_count // (4 * experts))
    slots = -(-3 * capacity // 16) * 16
    me = lax.axis_index("expert")
    lanes = -(-experts // 128) * 128
    names = jnp.arange(lanes, dtype=jnp.int32)
    table = jnp.sum(
        jnp.where(routes[:, :, None] == names[None, None, :], probs[:, :, None], 0.0), axis=1
    )
    rows, cot, table = gather_all(n_expert, n_dp, tokens, cotangent, table)
    weight = column(table, me)
    grads = scaled(cot, weight)
    gate = jnp.dot(rows, w_gate, preferred_element_type=jnp.float32)
    upper = jnp.dot(rows, w_up, preferred_element_type=jnp.float32)
    sig = jax.nn.sigmoid(gate)
    hidden = (gate * sig * upper).astype(jnp.bfloat16)
    hidden_back = jnp.dot(grads, w_down, preferred_element_type=jnp.float32)
    up_back = (hidden_back * gate * sig).astype(jnp.bfloat16)
    gate_back = (hidden_back * upper * sig * (1.0 + gate * (1.0 - sig))).astype(jnp.bfloat16)
    cubes = [v.reshape(experts, tok_rows, hidden_width) for v in (gate_back, up_back, hidden)]
    stacked = jnp.concatenate(cubes, axis=1)
    pick = selector(weight, experts, capacity, 3, slots)
    packed = jnp.einsum(
        "jrt,jth->jrh", pick, stacked, preferred_element_type=jnp.float32
    ).astype(jnp.bfloat16)
    landed, input_grad = exchange(
        n_expert, n_dp, matching, packed, gate_back, up_back, w_gate, w_up, tok_rows, tokens.shape[1]
    )
    partner = jnp.sum(jnp.where(jnp.arange(experts) == me, matching, 0))
    p_weight = column(table, partner)
    p_pick = selector(p_weight, experts, capacity, 3, slots)
    dense = jnp.einsum(
        "jrt,jrh->jth", p_pick, landed, preferred_element_type=jnp.float32
    ).astype(jnp.bfloat16)
    p_grads = scaled(cot, p_weight)
    total = experts * tok_rows

    def take(kind):
        return dense[:, kind * tok_rows : (kind + 1) * tok_rows].reshape(total, hidden_width)

    g_gate = lax.dot_general(rows, take(0), contract_rows, preferred_element_type=jnp.float32)
    g_up = lax.dot_general(rows, take(1), contract_rows, preferred_element_type=jnp.float32)
    g_down = lax.dot_general(p_grads, take(2), contract_rows, preferred_element_type=jnp.float32)
    return (input_grad, g_gate[None], g_up[None], g_down[None])


def solution(mesh):
    weights = P("expert", None, "dp")
    return jax.shard_map(
        functools.partial(local, mesh.shape["expert"], mesh.shape["dp"]),
        mesh=mesh,
        in_specs=(
            P("expert", "dp"),
            P("expert", "dp"),
            P("expert", None),
            P("expert", None),
            P(),
            weights,
            weights,
            weights,
        ),
        out_specs=(P("expert", "dp"), weights, weights, weights),
        check_vma=False,
    )
```
